256 devices in a mesh: dom: 8 (over z), feat: 32 (over y, x, core).
Axes of the slice: x: 4, y: 4, z: 8, core: 2. Of those that a mesh axis runs over, the one named last changes fastest.
Arguments:
- features: bfloat16 [32768, 4096], P('dom', 'feat'), may hold values from -6 to 6
- proj_weight: bfloat16 [3, 4096, 256], P(None, 'feat'), may hold values from -0.75 to 0.75
- source_block: int32 [256, 3, 4], P('dom'), may hold values from 0 to 31
- slot_count: int32 [256, 3], P('dom'), may hold values from 1 to 4
- block_pattern: int32 [256, 3, 4, 8, 128], P('dom'), may hold values from 0 to 65535
- node_type: int32 [32768], P(('dom', 'feat')), may hold values from 0 to 2
- type_gain: float32 [3, 256], replicated, may hold values from 0.1 to 1.9
- cotangent: bfloat16 [32768, 256], P(('dom', 'feat')), may hold values from -6 to 6
Outputs:
- activations: bfloat16 [32768, 256], P(('dom', 'feat'))
- weight_grad: float32 [3, 4096, 256], P(None, 'feat')
The draws below stay inside these ranges and needn't reach their ends.
Inputs may be any that keep to these rules, and one draw needn't show every extreme that they name: `source_block`: a block index within the destination block's own partition. `slot_count`: slots at or past this count are ignored. `block_pattern`: bit j of the word at index w, i marks an edge from source node 16 w + j of the slot's block to node i of the destination block.
All inputs are finite; a program needn't handle non-finite values.
Results may differ from the reference program's by a relative error of at most 0.0055.
Values may be sent and summed in bfloat16 or wider, within the bound.
A program may use at most 128 MiB of HBM per device.

```python
import jax
import jax.numpy as jnp
from jax import lax

IN_DIM = 4096
HID_DIM = 256
REL = 3
NTYPES = 3
SLOTS = 4
BLK = 128
WORDS = 8
PB = 32
PART_NODES = 4096
NODES = 32768
NBLK = 256
N_DOM = 8


def place_ends(values, own_key, least, top_value):
    dims = values.shape
    index_at = [jax.random.randint(jax.random.fold_in(own_key, axis), (), 0, dims[axis]) for axis in range(len(dims))]
    values = values.at[tuple(index_at)].set(least)
    longest = dims.index(max(dims))
    index_at[longest] = (index_at[longest] + 1) % dims[longest]
    return values.at[tuple(index_at)].set(top_value)


def shard_levels(own_key, shape, split, least, high):
    factor_of, own = 1.0, jax.random.fold_in(own_key, 6)
    for dim, blocks in split:
        draws = jnp.exp(jax.random.uniform(jax.random.fold_in(own, dim), (blocks,), jnp.float32, least / len(split), high / len(split)))
        factor_of = factor_of * jnp.repeat(draws, shape[dim] // blocks).reshape([-1 if axis == dim else 1 for axis in range(len(shape))])
    return factor_of


def scatter_about(own_key, shape, scale, limit, pieces=(), kind=jnp.bfloat16):
    array = scale * jax.random.normal(own_key, shape, jnp.float32)
    if pieces:
        array = array * shard_levels(own_key, shape, pieces, -0.22, 0.18)
    return jnp.clip(array, -limit, limit).astype(kind)


def setup_inputs(seed: int = 0) -> dict:
    arg_keys = jax.random.split(jax.random.key(seed), 9)
    return {
        "features": scatter_about(arg_keys[0], (NODES, IN_DIM), 1.0, 6.0, ((0, 8), (1, 32))),
        "proj_weight": scatter_about(arg_keys[1], (REL, IN_DIM, HID_DIM), (IN_DIM // 64) ** -0.5, 0.75, ((1, 32),)),
        "source_block": place_ends(jax.random.randint(arg_keys[2], (NBLK, REL, SLOTS), 0, PB), jax.random.fold_in(arg_keys[2], 1), 0, PB - 1).astype(jnp.int32),
        "slot_count": place_ends(jax.random.randint(arg_keys[3], (NBLK, REL), 1, SLOTS + 1), jax.random.fold_in(arg_keys[3], 1), 1, SLOTS).astype(jnp.int32),
        "block_pattern": place_ends(jax.random.randint(arg_keys[4], (NBLK, REL, SLOTS, WORDS, BLK), 0, 65536), jax.random.fold_in(arg_keys[4], 1), 0, 65535).astype(jnp.int32),
        "node_type": place_ends(jax.random.randint(arg_keys[5], (NODES,), 0, NTYPES), jax.random.fold_in(arg_keys[5], 1), 0, NTYPES - 1).astype(jnp.int32),
        "type_gain": jnp.clip(1.0 + 0.18 * jax.random.normal(arg_keys[6], (NTYPES, HID_DIM), jnp.float32), 0.1, 1.9),
        "cotangent": scatter_about(arg_keys[7], (NODES, HID_DIM), 1.0, 6.0, ((0, 256),)),
    }


def unpack_bits(packed):
    shifts = (2 ** jnp.arange(16)).astype(jnp.int32)
    bit_values = packed[..., None] // shifts % 2
    bit_values = jnp.swapaxes(bit_values, -3, -2)
    return bit_values.reshape(packed.shape[:-2] + (packed.shape[-1], packed.shape[-2] * 16))

def silu_grad(pre_act):
    sigmoid_value = jax.nn.sigmoid(pre_act)
    return sigmoid_value * (1.0 + pre_act * (1.0 - sigmoid_value))

def type_rows(node_type, type_gain):
    onehot = (node_type[:, None] == jnp.arange(type_gain.shape[0], dtype=jnp.int32)[None, :]).astype(jnp.float32)
    return lax.optimization_barrier(jnp.sum(onehot[:, :, None] * type_gain[None, :, :], axis=1))

def one_partition(partition_item, proj_weight, type_gain):
    features, source_block, slot_count, block_pattern, node_type, cotangent = partition_item
    blocks = features.reshape(PB, BLK, IN_DIM).astype(jnp.float32)
    live_slots = (jnp.arange(SLOTS, dtype=jnp.int32)[None, None, :] < slot_count[:, :, None]).astype(jnp.float32)
    pre_act = jnp.zeros((PART_NODES, HID_DIM), jnp.float32)
    mixed_list = []
    for relation in range(REL):
        summed = jnp.zeros((PB, BLK, IN_DIM), jnp.float32)
        degree = jnp.zeros((PB, BLK), jnp.float32)
        for slot_index in range(SLOTS):
            adjacency = unpack_bits(block_pattern[:, relation, slot_index]).astype(jnp.float32) * live_slots[:, relation, slot_index][:, None, None]
            picked = jnp.take(blocks, source_block[:, relation, slot_index].astype(jnp.int32), axis=0)
            summed = summed + jnp.einsum('bij,bjc->bic', adjacency, picked, precision=lax.Precision.HIGHEST)
            degree = degree + lax.optimization_barrier(jnp.sum(adjacency, axis=2))
        mixed_rows = ((blocks + summed) / (1.0 + degree)[:, :, None]).astype(jnp.bfloat16).reshape(PART_NODES, IN_DIM)
        mixed_list.append(mixed_rows)
        pre_act = pre_act + jnp.dot(mixed_rows, proj_weight[relation], preferred_element_type=jnp.float32)
    row_gains = type_rows(node_type, type_gain)
    output = (jax.nn.silu(pre_act) * row_gains).astype(jnp.bfloat16)
    slope_rows = (cotangent.astype(jnp.float32) * row_gains * silu_grad(pre_act)).astype(jnp.bfloat16)
    weight_grads = jnp.stack([jnp.dot(mixed_one.T, slope_rows, preferred_element_type=jnp.float32) for mixed_one in mixed_list])
    return (output, weight_grads)

def reference(features, proj_weight, source_block, slot_count, block_pattern, node_type, type_gain, cotangent):
    partition_items = (features.reshape(N_DOM, PART_NODES, IN_DIM), source_block.reshape(N_DOM, PB, REL, SLOTS), slot_count.reshape(N_DOM, PB, REL), block_pattern.reshape(N_DOM, PB, REL, SLOTS, WORDS, BLK), node_type.reshape(N_DOM, PART_NODES), cotangent.reshape(N_DOM, PART_NODES, HID_DIM))
    outputs, weight_grads = lax.map(lambda partition_item: one_partition(partition_item, proj_weight, type_gain), partition_items)
    return (outputs.reshape(NODES, HID_DIM), lax.optimization_barrier(jnp.sum(weight_grads, axis=0)))
```

```python
import functools

import jax
import jax.numpy as jnp
from jax import lax
from jax.experimental import pallas as pl
from jax.experimental.pallas import tpu as pltpu
from jax.sharding import PartitionSpec as P

MESH = pl.DeviceIdType.MESH
F32 = jnp.float32
BF16 = jnp.bfloat16
BLK = 128
REL = 3
SLOTS = 4
PB = 32
HID = 256
NZ = 8
PART = REL * BLK // NZ


def kernel(
    feat_ref,
    weight_ref,
    source_ref,
    count_ref,
    pattern_ref,
    type_ref,
    gain_ref,
    cot_ref,
    act_ref,
    grad_ref,
    self_t,
    perm_t,
    weight_t,
    mixed_t,
    own_part,
    pair_out,
    pair_in,
    rs_out,
    rs_in,
    slope_all,
    grad_acc,
    wg_out,
    wg_in,
    wg_all,
    pair_send,
    pair_recv,
    rs_send,
    rs_recv,
    agx_send,
    agx_recv,
    agy_send,
    agy_recv,
    core_send,
    core_recv,
    zs_send,
    zs_recv,
    zb_send,
    zb_recv,
):
    dom = lax.axis_index("dom")
    me = lax.axis_index("feat")
    core = me % 2
    chip = me // 2
    x = chip % 4
    y = chip // 4
    partner = me + 1 - 2 * core

    def at_feat(dest):
        return (dom, dest)

    def device_at(dy, dx):
        return (((y + dy) % 4) * 4 + (x + dx) % 4) * 2 + core

    barrier = pltpu.get_barrier_semaphore()

    def greet(dest):
        pl.semaphore_signal(barrier, inc=1, device_id=dest, device_id_type=MESH)

    greet(at_feat(partner))
    for off in range(1, 16):
        greet(at_feat(device_at(off // 4, off % 4)))
    for dz in range(1, NZ):
        greet(((dom + dz) % NZ, me))

    row = lax.broadcasted_iota(jnp.int32, (BLK, BLK), 0)
    col = lax.broadcasted_iota(jnp.int32, (BLK, BLK), 1)
    scale = 1.0 / (jnp.int32(1) << (col // 8)).astype(F32)
    perm = jnp.where(row == (col % 8) * 16 + col // 8, scale, 0.0).astype(BF16)
    eye = jnp.where(row == col, 1.0, 0.0).astype(BF16)

    for r in range(REL):
        for half in range(2):
            piece = weight_ref[r, :, half * BLK:(half + 1) * BLK]
            weight_t[half * BLK:(half + 1) * BLK, r * BLK:(r + 1) * BLK] = (
                piece.astype(F32).T.astype(BF16)
            )

    def prepare(i, carry):
        for k in range(4):
            b = i * 4 + k
            rows = feat_ref[pl.ds(pl.multiple_of(b * BLK, BLK), BLK), :]
            flipped = lax.dot_general(
                eye, rows, (((1,), (1,)), ((), ())), preferred_element_type=F32
            ).astype(BF16)
            self_t[b] = flipped
            perm_t[b] = jnp.dot(flipped, perm, preferred_element_type=F32).astype(BF16)
        return carry

    lax.fori_loop(0, PB // 4, prepare, 0)

    def mix(b):
        own_rows = self_t[b].astype(F32)
        for r in range(REL):
            count = count_ref[b, r]
            tiles = []
            gathered = []
            degree = None
            for s in range(SLOTS):
                words = pattern_ref[b, r, s]
                if s > 0:
                    words = words & jnp.where(s < count, jnp.int32(65535), jnp.int32(0))
                bits = lax.population_count(words)
                degree = bits if degree is None else degree + bits
                for j in range(16):
                    tiles.append((words & (1 << j)).astype(F32))
                gathered.append(perm_t[source_ref[b, r, s]])
            adj = jnp.concatenate(tiles, axis=0).astype(BF16)
            sources = jnp.concatenate(gathered, axis=1)
            summed = jnp.dot(sources, adj, preferred_element_type=F32)
            total = 1.0 + jnp.sum(degree.astype(F32), axis=0, keepdims=True)
            mixed_t[b, r * BLK:(r + 1) * BLK, :] = ((own_rows + summed) * (1.0 / total)).astype(BF16)

    def pair_copy(step):
        return pltpu.make_async_remote_copy(
            src_ref=pair_out.at[step],
            dst_ref=pair_in.at[step],
            send_sem=pair_send.at[step],
            recv_sem=pair_recv.at[step],
            device_id=at_feat(partner),
            device_id_type=MESH,
        )

    def rs_copy(step):
        off = 15 - step
        return pltpu.make_async_remote_copy(
            src_ref=rs_out.at[step],
            dst_ref=rs_in.at[step],
            send_sem=rs_send.at[step],
            recv_sem=rs_recv.at[step],
            device_id=at_feat(device_at(off // 4, off % 4)),
            device_id_type=MESH,
        )

    def project(step):
        off = 15 - step
        mine = device_at(off // 4, off % 4)
        other = mine + 1 - 2 * core
        mix(mine)
        mix(other)
        both = jnp.concatenate([mixed_t[mine], mixed_t[other]], axis=1)
        part = jnp.dot(weight_t[...], both, preferred_element_type=F32)
        own_part[step % 2] = part[:, :BLK]
        pair_out[step] = part[:, BLK:].astype(BF16)

    def pair_sum(step):
        pair_copy(step).wait_recv()
        return own_part[step % 2] + pair_in[step].astype(F32)

    project(0)
    pl.semaphore_wait(barrier, 1 + 15 + NZ - 1)
    pair_copy(0).start()

    def stage(step, carry):
        project(step)
        pair_copy(step).start()
        rs_out[step - 1] = pair_sum(step - 1).astype(BF16)
        rs_copy(step - 1).start()
        return carry

    lax.fori_loop(1, 16, stage, 0)
    total = pair_sum(15)
    for step in range(15):
        rs_copy(step).wait_recv()
        total = total + rs_in[step].astype(F32)

    types = jnp.broadcast_to(type_ref[...].astype(F32), (BLK, BLK)).T
    for half in range(2):
        cols = slice(half * BLK, (half + 1) * BLK)
        pre = total[cols].T
        gains = gain_ref[:, cols]
        gain = jnp.where(types == 0.0, gains[0:1], jnp.where(types == 1.0, gains[1:2], gains[2:3]))
        sig = jax.nn.sigmoid(pre)
        act_ref[:, cols] = (pre * sig * gain).astype(BF16)
        slope = cot_ref[:, cols].astype(F32) * gain * (sig * (1.0 + pre * (1.0 - sig)))
        slope_all[me, :, cols] = slope.astype(BF16)

    def to_core(block, slot):
        return pltpu.make_async_remote_copy(
            src_ref=slope_all.at[block],
            dst_ref=slope_all.at[block],
            send_sem=core_send.at[slot],
            recv_sem=core_recv.at[slot],
            device_id=at_feat(partner),
            device_id_type=MESH,
        )

    def over_x(block, line, dx):
        return pltpu.make_async_remote_copy(
            src_ref=slope_all.at[block, pl.ds(64 if line[1] else 0, 64)],
            dst_ref=slope_all.at[block, pl.ds(64 if line[1] else 0, 64)],
            send_sem=agx_send.at[line[0] + 4 * line[1], dx],
            recv_sem=agx_recv.at[line[0] + 4 * line[1], dx],
            device_id=at_feat(device_at(0, dx)),
            device_id_type=MESH,
        )

    def over_y(block, line, dy):
        return pltpu.make_async_remote_copy(
            src_ref=slope_all.at[block, pl.ds(0 if line[1] else 64, 64)],
            dst_ref=slope_all.at[block, pl.ds(0 if line[1] else 64, 64)],
            send_sem=agy_send.at[line[0] + 4 * line[1], dy],
            recv_sem=agy_recv.at[line[0] + 4 * line[1], dy],
            device_id=at_feat(device_at(dy, 0)),
            device_id_type=MESH,
        )

    hops = (1, 3, 2)
    for d in hops:
        over_x(me, (0, 0), d).start()
        over_y(me, (0, 0), d).start()
    for d in hops:
        over_x(me, (0, 1), d).start()
        over_y(me, (0, 1), d).start()
    to_core(me, 0).start()
    for d in hops:
        across = device_at(0, 4 - d)
        over_x(across, (0, 0), d).wait_recv()
        for e in hops:
            over_y(across, (d, 1), e).start()
        down = device_at(4 - d, 0)
        over_y(down, (0, 0), d).wait_recv()
        for e in hops:
            over_x(down, (d, 1), e).start()

    def arrived(dy, dx):
        block = device_at(4 - dy, 4 - dx)
        if dy == 0:
            over_x(block, (0, 1), dx).wait_recv()
        elif dx == 0:
            over_y(block, (0, 1), dy).wait_recv()
        else:
            over_y(block, (dx, 1), dy).wait_recv()
            over_x(block, (dy, 1), dx).wait_recv()
        return block

    def add_grad(block, slot):
        twin = block + 1 - 2 * core
        to_core(twin, slot).wait_recv()
        lhs = jnp.concatenate([mixed_t[block], mixed_t[twin]], axis=1)
        rhs = jnp.concatenate([slope_all[block], slope_all[twin]], axis=0)
        return jnp.dot(lhs, rhs, preferred_element_type=F32)

    order = [(0, 1), (0, 3), (1, 0), (3, 0), (0, 2), (2, 0), (1, 1), (1, 3), (3, 1), (3, 3),
             (1, 2), (2, 1), (3, 2), (2, 3), (2, 2)]
    before = (me, 0)
    for n, (dy, dx) in enumerate(order):
        block = arrived(dy, dx)
        to_core(block, dy * 4 + dx).start()
        if n == 0:
            grad_acc[...] = add_grad(*before)
        else:
            grad_acc[...] += add_grad(*before)
        before = (block, dy * 4 + dx)
    grad_acc[...] += add_grad(*before)

    def scatter(dz):
        return pltpu.make_async_remote_copy(
            src_ref=wg_out.at[(dom + dz) % NZ],
            dst_ref=wg_in.at[dz],
            send_sem=zs_send.at[dz],
            recv_sem=zs_recv.at[dz],
            device_id=((dom + dz) % NZ, me),
            device_id_type=MESH,
        )

    def spread(dz, part):
        return pltpu.make_async_remote_copy(
            src_ref=wg_all.at[part],
            dst_ref=wg_all.at[part],
            send_sem=zb_send.at[dz],
            recv_sem=zb_recv.at[dz],
            device_id=((dom + dz) % NZ, me),
            device_id_type=MESH,
        )

    for p in range(NZ):
        wg_out[p] = grad_acc[p * PART:(p + 1) * PART, :].astype(BF16)
    zorder = (4, 3, 5, 2, 6, 1, 7)
    for dz in zorder:
        scatter(dz).start()
    own = grad_acc[pl.ds(pl.multiple_of(dom * PART, 8), PART), :]
    for dz in reversed(zorder):
        scatter(dz).wait_recv()
        own = own + wg_in[dz].astype(F32)
    wg_all[dom] = own.astype(BF16)
    for dz in zorder:
        spread(dz, dom).start()
    grad_ref[pl.ds(pl.multiple_of(dom * PART, 8), PART), :] = own.astype(BF16).astype(F32)
    for dz in reversed(zorder):
        part = (dom + NZ - dz) % NZ
        spread(dz, part).wait_recv()
        grad_ref[pl.ds(pl.multiple_of(part * PART, 8), PART), :] = wg_all[part].astype(F32)

    def drain(step, carry):
        pair_copy(step).wait_send()
        return carry

    lax.fori_loop(0, 16, drain, 0)

    def drain_rs(step, carry):
        rs_copy(step).wait_send()
        return carry

    lax.fori_loop(0, 15, drain_rs, 0)
    for d in hops:
        over_x(me, (0, 0), d).wait_send()
        over_y(me, (0, 0), d).wait_send()
        for k in range(4):
            over_x(me, (k, 1), d).wait_send()
            over_y(me, (k, 1), d).wait_send()
    for slot in range(16):
        to_core(me, slot).wait_send()
    for dz in range(1, NZ):
        scatter(dz).wait_send()
        spread(dz, dom).wait_send()


def body(
    features, proj_weight, source_block, slot_count, block_pattern, node_type, type_gain, cotangent
):
    vmem = pl.BlockSpec(memory_space=pltpu.VMEM)
    smem = pl.BlockSpec(memory_space=pltpu.SMEM)
    activations, grad = pl.pallas_call(
        kernel,
        out_shape=(
            jax.ShapeDtypeStruct((BLK, HID), BF16),
            jax.ShapeDtypeStruct((REL * BLK, HID), F32),
        ),
        in_specs=[vmem, vmem, smem, smem, vmem, vmem, vmem, vmem],
        out_specs=(vmem, vmem),
        scratch_shapes=[
            pltpu.VMEM((PB, BLK, BLK), BF16),
            pltpu.VMEM((PB, BLK, BLK), BF16),
            pltpu.VMEM((HID, REL * BLK), BF16),
            pltpu.VMEM((PB, REL * BLK, BLK), BF16),
            pltpu.VMEM((2, HID, BLK), F32),
            pltpu.VMEM((16, HID, BLK), BF16),
            pltpu.VMEM((16, HID, BLK), BF16),
            pltpu.VMEM((16, HID, BLK), BF16),
            pltpu.VMEM((16, HID, BLK), BF16),
            pltpu.VMEM((PB, BLK, HID), BF16),
            pltpu.VMEM((REL * BLK, HID), F32),
            pltpu.VMEM((NZ, PART, HID), BF16),
            pltpu.VMEM((NZ, PART, HID), BF16),
            pltpu.VMEM((NZ, PART, HID), BF16),
            pltpu.SemaphoreType.DMA((16,)),
            pltpu.SemaphoreType.DMA((16,)),
            pltpu.SemaphoreType.DMA((16,)),
            pltpu.SemaphoreType.DMA((16,)),
            pltpu.SemaphoreType.DMA((8, 4)),
            pltpu.SemaphoreType.DMA((8, 4)),
            pltpu.SemaphoreType.DMA((8, 4)),
            pltpu.SemaphoreType.DMA((8, 4)),
            pltpu.SemaphoreType.DMA((16,)),
            pltpu.SemaphoreType.DMA((16,)),
            pltpu.SemaphoreType.DMA((NZ,)),
            pltpu.SemaphoreType.DMA((NZ,)),
            pltpu.SemaphoreType.DMA((NZ,)),
            pltpu.SemaphoreType.DMA((NZ,)),
        ],
        compiler_params=pltpu.CompilerParams(
            collective_id=0, has_side_effects=True, vmem_limit_bytes=60 * 1024 * 1024
        ),
        name="graph_conv",
    )(
        features,
        proj_weight,
        source_block,
        slot_count,
        block_pattern,
        node_type.reshape(1, BLK),
        type_gain,
        cotangent,
    )
    return activations, grad.reshape(REL, BLK, HID)


def solution(mesh):
    placed = (
        P("dom", "feat"),
        P(None, "feat", None),
        P("dom", None, None),
        P("dom", None),
        P("dom", None, None, None, None),
        P(("dom", "feat")),
        P(),
        P(("dom", "feat"), None),
    )
    return jax.shard_map(
        body,
        mesh=mesh,
        in_specs=placed,
        out_specs=(P(("dom", "feat"), None), P(None, "feat", None)),
        check_vma=False,
    )
```

```python
import functools

import jax
import jax.numpy as jnp
from jax import lax
from jax.experimental import pallas as pl
from jax.experimental.pallas import tpu as pltpu
from jax.sharding import PartitionSpec as P

MESH = pl.DeviceIdType.MESH
F32 = jnp.float32
BF16 = jnp.bfloat16
BLK = 128
REL = 3
NTYPES = 3
SLOTS = 4
PB = 32
HID = 256
NZ = 8
DXS = (2, 3, 1, 0)
PART = REL * BLK // NZ


def kernel(
    feat_hbm,
    weight_hbm,
    source_hbm,
    count_hbm,
    pattern_hbm,
    type_hbm,
    gain_hbm,
    cot_hbm,
    act_ref,
    wg_all,
    feat_ref,
    weight_ref,
    source_ref,
    count_ref,
    pattern_ref,
    type_ref,
    gain_ref,
    cot_ref,
    load_sem,
    self_t,
    perm_t,
    weight_t,
    mixed_t,
    own_part,
    keep_top,
    pair_out,
    pair_in,
    x_out,
    x_in,
    y_out,
    y_in,
    turn_out,
    turn_in,
    slope_all,
    grad_acc,
    wg_out,
    wg_in,
    pair_send,
    pair_recv,
    x_send,
    x_recv,
    y_send,
    y_recv,
    turn_send,
    turn_recv,
    agx_send,
    agx_recv,
    agy_send,
    agy_recv,
    core_send,
    core_recv,
    zs_send,
    zs_recv,
    zb_send,
    zb_recv,
):
    dom = lax.axis_index("dom")
    me = lax.axis_index("feat")
    core = me % 2
    chip = me // 2
    x = chip % 4
    y = chip // 4
    partner = me + 1 - 2 * core

    def at_feat(dest):
        return (dom, dest)

    def device_at(dy, dx):
        return (((y + dy) % 4) * 4 + (x + dx) % 4) * 2 + core

    loads = [
        pltpu.make_async_copy(src, dst, load_sem.at[n])
        for n, (src, dst) in enumerate((
            (feat_hbm, feat_ref),
            (weight_hbm, weight_ref),
            (source_hbm, source_ref),
            (count_hbm, count_ref),
            (pattern_hbm, pattern_ref),
            (type_hbm, type_ref),
            (gain_hbm, gain_ref),
            (cot_hbm, cot_ref),
        ))
    ]
    for load in loads:
        load.start()

    barrier = pltpu.get_barrier_semaphore()

    def greet(dest):
        pl.semaphore_signal(barrier, inc=1, device_id=dest, device_id_type=MESH)

    greet(at_feat(partner))
    for off in range(1, 16):
        greet(at_feat(device_at(off // 4, off % 4)))
    for dz in range(1, NZ):
        greet(((dom + dz) % NZ, me))

    row = lax.broadcasted_iota(jnp.int32, (BLK, BLK), 0)
    col = lax.broadcasted_iota(jnp.int32, (BLK, BLK), 1)
    scale = 1.0 / (jnp.int32(1) << (col // 8)).astype(F32)
    perm = jnp.where(row == (col % 8) * 16 + col // 8, scale, 0.0).astype(BF16)
    eye = jnp.where(row == col, 1.0, 0.0).astype(BF16)

    loads[0].wait()
    loads[1].wait()
    for r in range(REL):
        for half in range(2):
            piece = weight_ref[r, :, half * BLK:(half + 1) * BLK]
            weight_t[half * BLK:(half + 1) * BLK, r * BLK:(r + 1) * BLK] = (
                piece.astype(F32).T.astype(BF16)
            )

    def prepare(i, carry):
        for k in range(4):
            b = i * 4 + k
            rows = feat_ref[pl.ds(pl.multiple_of(b * BLK, BLK), BLK), :]
            flipped = lax.dot_general(
                eye, rows, (((1,), (1,)), ((), ())), preferred_element_type=F32
            ).astype(BF16)
            self_t[b] = flipped
            perm_t[b] = jnp.dot(flipped, perm, preferred_element_type=F32).astype(BF16)
        return carry

    lax.fori_loop(0, PB // 4, prepare, 0)
    for load in loads[2:]:
        load.wait()

    def mix(b):
        own_rows = self_t[b].astype(F32)
        for r in range(REL):
            count = count_ref[r, b]
            tiles = []
            gathered = []
            degree = None
            for s in range(SLOTS):
                words = pattern_ref[b, r, s]
                if s > 0:
                    words = words & jnp.where(s < count, jnp.int32(65535), jnp.int32(0))
                bits = lax.population_count(words)
                degree = bits if degree is None else degree + bits
                for j in range(16):
                    tiles.append((words & (1 << j)).astype(F32))
                gathered.append(perm_t[source_ref[r, s, b]])
            adj = jnp.concatenate(tiles, axis=0).astype(BF16)
            sources = jnp.concatenate(gathered, axis=1)
            summed = jnp.dot(sources, adj, preferred_element_type=F32)
            total = 1.0 + jnp.sum(degree.astype(F32), axis=0, keepdims=True)
            mixed_t[b, r * BLK:(r + 1) * BLK, :] = ((own_rows + summed) * (1.0 / total)).astype(BF16)

    def pair_copy(step):
        return pltpu.make_async_remote_copy(
            src_ref=pair_out.at[step],
            dst_ref=pair_in.at[step],
            send_sem=pair_send.at[step],
            recv_sem=pair_recv.at[step],
            device_id=at_feat(partner),
            device_id_type=MESH,
        )

    def shift(n):
        return 2 + n - 3 * (n // 2) - 2 * (n // 3)

    def offset(step):
        group, k = step // 4, step % 4
        return shift(group), shift(k)

    def target(step):
        dy, dx = offset(step)
        return device_at(dy, dx)

    def x_copy(step, dx):
        return pltpu.make_async_remote_copy(
            src_ref=x_out.at[step],
            dst_ref=x_in.at[step],
            send_sem=x_send.at[step],
            recv_sem=x_recv.at[step],
            device_id=at_feat(device_at(0, dx)),
            device_id_type=MESH,
        )

    def y_copy(step, dy):
        return pltpu.make_async_remote_copy(
            src_ref=y_out.at[step],
            dst_ref=y_in.at[step],
            send_sem=y_send.at[step],
            recv_sem=y_recv.at[step],
            device_id=at_feat(device_at(dy, 0)),
            device_id_type=MESH,
        )

    def turn_copy(kind, slot, d):
        return pltpu.make_async_remote_copy(
            src_ref=turn_out.at[kind, slot],
            dst_ref=turn_in.at[kind, slot],
            send_sem=turn_send.at[kind, slot],
            recv_sem=turn_recv.at[kind, slot],
            device_id=at_feat(device_at(d, 0) if kind == 0 else device_at(0, d)),
            device_id_type=MESH,
        )

    def project(step):
        mine = target(step)
        other = mine + 1 - 2 * core
        mix(mine)
        mix(other)
        both = jnp.concatenate([mixed_t[mine], mixed_t[other]], axis=1)
        part = jnp.dot(weight_t[...], both, preferred_element_type=F32)
        own_part[step] = part[:, :BLK]
        pair_out[step] = part[:, BLK:].astype(BF16)
        pair_copy(step).start()

    def top_sum(step):
        return own_part[step, :BLK] + pair_in[step, :BLK].astype(F32)

    def low_sum(step):
        return own_part[step, BLK:] + pair_in[step, BLK:].astype(F32)

    def send_top(step, k):
        x_out[step] = top_sum(step).astype(BF16)
        x_copy(step, DXS[k]).start()

    def send_low(step, dy):
        y_out[step] = low_sum(step).astype(BF16)
        y_copy(step, dy).start()

    def row_sum(group, mine):
        for k in range(3):
            x_copy(4 * group + k, DXS[k]).wait_recv()
            mine = mine + x_in[4 * group + k].astype(F32)
        return mine

    def send_row(group, dy):
        turn_out[0, group] = row_sum(group, keep_top[group]).astype(BF16)
        turn_copy(0, group, dy).start()

    def column_sum(k, mine):
        for group in range(3):
            y_copy(4 * group + k, 1).wait_recv()
            mine = mine + y_in[4 * group + k].astype(F32)
        return mine

    pl.semaphore_wait(barrier, 1 + 15 + NZ - 1)
    project(0)
    project(1)

    def four(group, carry):
        dy = shift(group)
        for k in range(4):
            step = 4 * group + k
            project(step + 2)
            pair_copy(step).wait_recv()
            if k < 3:
                send_top(step, k)
            else:
                keep_top[group] = top_sum(step)
            send_low(step, dy)
            if k == 2:
                @pl.when(group > 0)
                def _():
                    send_row(group - 1, shift(group - 1))
        return carry

    lax.fori_loop(0, 3, four, 0)
    for k in range(4):
        step = 12 + k
        if k < 2:
            project(step + 2)
        pair_copy(step).wait_recv()
        if k < 3:
            send_top(step, k)
            turn_out[1, k] = column_sum(k, low_sum(step)).astype(BF16)
            turn_copy(1, k, DXS[k]).start()
        if k == 2:
            send_row(2, 1)
    top = row_sum(3, top_sum(15))
    low = column_sum(3, low_sum(15))
    for slot in range(3):
        turn_copy(0, slot, 1).wait_recv()
        top = top + turn_in[0, slot].astype(F32)
        turn_copy(1, slot, 1).wait_recv()
        low = low + turn_in[1, slot].astype(F32)

    types = jnp.broadcast_to(type_ref[...].astype(F32), (BLK, BLK)).T
    for half in range(2):
        cols = slice(half * BLK, (half + 1) * BLK)
        pre = (top, low)[half].T
        gains = gain_ref[:, cols]
        gain = jnp.where(types == 0.0, gains[0:1], jnp.where(types == 1.0, gains[1:2], gains[2:3]))
        sig = jax.nn.sigmoid(pre)
        act_ref[:, cols] = (pre * sig * gain).astype(BF16)
        slope = cot_ref[:, cols].astype(F32) * gain * (sig * (1.0 + pre * (1.0 - sig)))
        slope_all[half, me] = slope.astype(BF16)

    def to_core(half, block, slot):
        return pltpu.make_async_remote_copy(
            src_ref=slope_all.at[half, block],
            dst_ref=slope_all.at[half, block],
            send_sem=core_send.at[half, slot],
            recv_sem=core_recv.at[half, slot],
            device_id=at_feat(partner),
            device_id_type=MESH,
        )

    def over_x(half, block, line, dx):
        rows = pl.ds(64 if line > 0 else 0, 64)
        return pltpu.make_async_remote_copy(
            src_ref=slope_all.at[half, block, rows],
            dst_ref=slope_all.at[half, block, rows],
            send_sem=agx_send.at[half, line, dx],
            recv_sem=agx_recv.at[half, line, dx],
            device_id=at_feat(device_at(0, dx)),
            device_id_type=MESH,
        )

    def over_y(half, block, line, dy):
        rows = pl.ds(0 if line > 0 else 64, 64)
        return pltpu.make_async_remote_copy(
            src_ref=slope_all.at[half, block, rows],
            dst_ref=slope_all.at[half, block, rows],
            send_sem=agy_send.at[half, line, dy],
            recv_sem=agy_recv.at[half, line, dy],
            device_id=at_feat(device_at(dy, 0)),
            device_id_type=MESH,
        )

    for half in range(2):
        for line in range(2):
            for d in DXS[:3]:
                over_x(half, me, line, d).start()
                over_y(half, me, line, d).start()
        to_core(half, me, 0).start()

    def forward(half):
        for d in (1, 3, 2):
            across = device_at(0, 4 - d)
            over_x(half, across, 0, d).wait_recv()
            for e in DXS[:3]:
                over_y(half, across, 1 + d, e).start()
            down = device_at(4 - d, 0)
            over_y(half, down, 0, d).wait_recv()
            for e in DXS[:3]:
                over_x(half, down, 1 + d, e).start()

    def arrived(half, dy, dx):
        block = device_at(4 - dy, 4 - dx)
        if dx > 0:
            over_x(half, block, 1 + dy, dx).wait_recv()
        if dy > 0:
            over_y(half, block, 1 + dx, dy).wait_recv()
        return block

    def add_grad(half, block, slot):
        twin = block + 1 - 2 * core
        to_core(half, twin, slot).wait_recv()
        lhs = jnp.concatenate([mixed_t[block], mixed_t[twin]], axis=1)
        rhs = jnp.concatenate([slope_all[half, block], slope_all[half, twin]], axis=0)
        return jnp.dot(lhs, rhs, preferred_element_type=F32)

    order = [(0, 1), (0, 3), (1, 0), (3, 0), (0, 2), (2, 0), (1, 1), (1, 3), (3, 1), (3, 3),
             (1, 2), (2, 1), (3, 2), (2, 3), (2, 2)]

    def relay(half):
        for dy, dx in order:
            block = arrived(half, dy, dx)
            to_core(half, block, dy * 4 + dx).start()

    def gradient(half):
        grad_acc[...] = add_grad(half, me, 0)
        for dy, dx in order:
            grad_acc[...] += add_grad(half, device_at(4 - dy, 4 - dx), dy * 4 + dx)

    def scatter(half, dz):
        return pltpu.make_async_remote_copy(
            src_ref=wg_out.at[half, (dom + dz) % NZ],
            dst_ref=wg_in.at[half, dz],
            send_sem=zs_send.at[half, dz],
            recv_sem=zs_recv.at[half, dz],
            device_id=((dom + dz) % NZ, me),
            device_id_type=MESH,
        )

    def spread(half, dz, part):
        return pltpu.make_async_remote_copy(
            src_ref=wg_all.at[half, part],
            dst_ref=wg_all.at[half, part],
            send_sem=zb_send.at[half, dz],
            recv_sem=zb_recv.at[half, dz],
            device_id=((dom + dz) % NZ, me),
            device_id_type=MESH,
        )

    zorder = (4, 3, 5, 2, 6, 1, 7)

    def scatter_all(half):
        for p in range(NZ):
            wg_out[half, p] = grad_acc[p * PART:(p + 1) * PART, :].astype(BF16)
        for dz in zorder:
            scatter(half, dz).start()
        return grad_acc[pl.ds(pl.multiple_of(dom * PART, 8), PART), :]

    def spread_all(half, own):
        for dz in reversed(zorder):
            scatter(half, dz).wait_recv()
            own = own + wg_in[half, dz].astype(F32)
        wg_all[half, dom] = own.astype(BF16)
        for dz in zorder:
            spread(half, dz, dom).start()

    forward(0)
    forward(1)
    relay(0)
    gradient(0)
    first = scatter_all(0)
    relay(1)
    gradient(1)
    second = scatter_all(1)
    spread_all(0, first)
    spread_all(1, second)

    def drain(step, carry):
        pair_copy(step).wait_send()
        return carry

    lax.fori_loop(0, 16, drain, 0)
    for step in range(16):
        if step % 4 < 3:
            x_copy(step, 1).wait_send()
        if step < 12:
            y_copy(step, 1).wait_send()
    for slot in range(3):
        turn_copy(0, slot, 1).wait_send()
        turn_copy(1, slot, 1).wait_send()
    for half in range(2):
        for d in range(1, 4):
            for line in range(5):
                over_x(half, me, line, d).wait_send()
                over_y(half, me, line, d).wait_send()
        for slot in range(16):
            to_core(half, me, slot).wait_send()
        for dz in range(1, NZ):
            scatter(half, dz).wait_send()
            spread(half, dz, dom).wait_send()
    for half in range(2):
        for dz in range(1, NZ):
            spread(half, dz, (dom + NZ - dz) % NZ).wait_recv()


def finish(act_in, wg_in, act_ref, grad_ref):
    act_ref[...] = act_in[...]
    for half in range(2):
        for p in range(NZ):
            grad_ref[p * PART:(p + 1) * PART, half * BLK:(half + 1) * BLK] = wg_in[half, p].astype(F32)


def body(
    features, proj_weight, source_block, slot_count, block_pattern, node_type, type_gain, cotangent
):
    vmem = pl.BlockSpec(memory_space=pltpu.VMEM)
    activations, parts = pl.pallas_call(
        kernel,
        out_shape=(
            jax.ShapeDtypeStruct((BLK, HID), BF16),
            jax.ShapeDtypeStruct((2, NZ, PART, BLK), BF16),
        ),
        in_specs=[pl.BlockSpec(memory_space=pl.ANY)] * 8,
        out_specs=(vmem, vmem),
        scratch_shapes=[
            pltpu.VMEM((PB * BLK, BLK), BF16),
            pltpu.VMEM((REL, BLK, HID), BF16),
            pltpu.SMEM((REL, SLOTS, PB), jnp.int32),
            pltpu.SMEM((REL, PB), jnp.int32),
            pltpu.VMEM((PB, REL, SLOTS, 8, BLK), jnp.int32),
            pltpu.VMEM((1, BLK), jnp.int32),
            pltpu.VMEM((NTYPES, HID), F32),
            pltpu.VMEM((BLK, HID), BF16),
            pltpu.SemaphoreType.DMA((8,)),
            pltpu.VMEM((PB, BLK, BLK), BF16),
            pltpu.VMEM((PB, BLK, BLK), BF16),
            pltpu.VMEM((HID, REL * BLK), BF16),
            pltpu.VMEM((PB, REL * BLK, BLK), BF16),
            pltpu.VMEM((16, HID, BLK), F32),
            pltpu.VMEM((3, BLK, BLK), F32),
            pltpu.VMEM((16, HID, BLK), BF16),
            pltpu.VMEM((16, HID, BLK), BF16),
            pltpu.VMEM((16, BLK, BLK), BF16),
            pltpu.VMEM((16, BLK, BLK), BF16),
            pltpu.VMEM((16, BLK, BLK), BF16),
            pltpu.VMEM((16, BLK, BLK), BF16),
            pltpu.VMEM((2, 3, BLK, BLK), BF16),
            pltpu.VMEM((2, 3, BLK, BLK), BF16),
            pltpu.VMEM((2, PB, BLK, BLK), BF16),
            pltpu.VMEM((REL * BLK, BLK), F32),
            pltpu.VMEM((2, NZ, PART, BLK), BF16),
            pltpu.VMEM((2, NZ, PART, BLK), BF16),
            pltpu.SemaphoreType.DMA((16,)),
            pltpu.SemaphoreType.DMA((16,)),
            pltpu.SemaphoreType.DMA((16,)),
            pltpu.SemaphoreType.DMA((16,)),
            pltpu.SemaphoreType.DMA((16,)),
            pltpu.SemaphoreType.DMA((16,)),
            pltpu.SemaphoreType.DMA((2, 3)),
            pltpu.SemaphoreType.DMA((2, 3)),
            pltpu.SemaphoreType.DMA((2, 5, 4)),
            pltpu.SemaphoreType.DMA((2, 5, 4)),
            pltpu.SemaphoreType.DMA((2, 5, 4)),
            pltpu.SemaphoreType.DMA((2, 5, 4)),
            pltpu.SemaphoreType.DMA((2, 16)),
            pltpu.SemaphoreType.DMA((2, 16)),
            pltpu.SemaphoreType.DMA((2, NZ)),
            pltpu.SemaphoreType.DMA((2, NZ)),
            pltpu.SemaphoreType.DMA((2, NZ)),
            pltpu.SemaphoreType.DMA((2, NZ)),
        ],
        compiler_params=pltpu.CompilerParams(
            collective_id=0, has_side_effects=True, vmem_limit_bytes=60 * 1024 * 1024
        ),
        name="graph_conv",
    )(
        features,
        proj_weight,
        jnp.transpose(source_block, (1, 2, 0)),
        jnp.transpose(slot_count, (1, 0)),
        block_pattern,
        node_type.reshape(1, BLK),
        type_gain,
        cotangent,
    )
    activations, grad = pl.pallas_call(
        finish,
        out_shape=(
            jax.ShapeDtypeStruct((BLK, HID), BF16),
            jax.ShapeDtypeStruct((REL * BLK, HID), F32),
        ),
        in_specs=[vmem, vmem],
        out_specs=(vmem, vmem),
        name="finish",
    )(activations, parts)
    return activations, grad.reshape(REL, BLK, HID)


def solution(mesh):
    placed = (
        P("dom", "feat"),
        P(None, "feat", None),
        P("dom", None, None),
        P("dom", None),
        P("dom", None, None, None, None),
        P(("dom", "feat")),
        P(),
        P(("dom", "feat"), None),
    )
    return jax.shard_map(
        body,
        mesh=mesh,
        in_specs=placed,
        out_specs=(P(("dom", "feat"), None), P(None, "feat", None)),
        check_vma=False,
    )
```

```python
import functools

import jax
import jax.numpy as jnp
from jax import lax
from jax.experimental import pallas as pl
from jax.experimental.pallas import tpu as pltpu
from jax.sharding import PartitionSpec as P

MESH = pl.DeviceIdType.MESH
F32 = jnp.float32
BF16 = jnp.bfloat16
BLK = 128
REL = 3
NTYPES = 3
SLOTS = 4
PB = 32
HID = 256
NZ = 8
DXS = (2, 3, 1, 0)
PART = REL * BLK // NZ


def kernel(
    feat_hbm,
    weight_hbm,
    source_hbm,
    count_hbm,
    pattern_hbm,
    type_hbm,
    gain_hbm,
    cot_hbm,
    act_ref,
    wg_all,
    feat_ref,
    weight_ref,
    source_ref,
    count_ref,
    pattern_ref,
    type_ref,
    gain_ref,
    cot_ref,
    load_sem,
    self_t,
    perm_t,
    weight_t,
    mixed_t,
    own_part,
    keep_top,
    pair_out,
    pair_in,
    x_out,
    x_in,
    y_out,
    y_in,
    turn_out,
    turn_in,
    slope_all,
    grad_acc,
    wg_out,
    wg_in,
    pair_send,
    pair_recv,
    x_send,
    x_recv,
    y_send,
    y_recv,
    turn_send,
    turn_recv,
    agx_send,
    agx_recv,
    agy_send,
    agy_recv,
    core_send,
    core_recv,
    zs_send,
    zs_recv,
    zb_send,
    zb_recv,
):
    dom = lax.axis_index("dom")
    me = lax.axis_index("feat")
    core = me % 2
    chip = me // 2
    x = chip % 4
    y = chip // 4
    partner = me + 1 - 2 * core

    def at_feat(dest):
        return (dom, dest)

    def device_at(dy, dx):
        return (((y + dy) % 4) * 4 + (x + dx) % 4) * 2 + core

    def piece_of(ref, n):
        return ref.at[pl.ds(n * 1024, 1024)]

    loads = [
        pltpu.make_async_copy(src, dst, load_sem.at[n])
        for n, (src, dst) in enumerate((
            (piece_of(feat_hbm, 0), piece_of(feat_ref, 0)),
            (piece_of(feat_hbm, 1), piece_of(feat_ref, 1)),
            (piece_of(feat_hbm, 2), piece_of(feat_ref, 2)),
            (piece_of(feat_hbm, 3), piece_of(feat_ref, 3)),
            (weight_hbm, weight_ref),
            (source_hbm, source_ref),
            (count_hbm, count_ref),
            (pattern_hbm, pattern_ref),
            (type_hbm, type_ref),
            (gain_hbm, gain_ref),
            (cot_hbm, cot_ref),
        ))
    ]
    for load in loads:
        load.start()

    barrier = pltpu.get_barrier_semaphore()

    def greet(dest):
        pl.semaphore_signal(barrier, inc=1, device_id=dest, device_id_type=MESH)

    greet(at_feat(partner))
    for d in range(1, 4):
        greet(at_feat(device_at(0, d)))
        greet(at_feat(device_at(d, 0)))
    for dz in range(1, NZ):
        greet(((dom + dz) % NZ, me))

    row = lax.broadcasted_iota(jnp.int32, (BLK, BLK), 0)
    col = lax.broadcasted_iota(jnp.int32, (BLK, BLK), 1)
    scale = 1.0 / (jnp.int32(1) << (col // 8)).astype(F32)
    perm = jnp.where(row == (col % 8) * 16 + col // 8, scale, 0.0).astype(BF16)
    eye = jnp.where(row == col, 1.0, 0.0).astype(BF16)

    for n in range(4):
        loads[n].wait()
        flipped = lax.dot_general(
            eye,
            feat_ref[n * 1024:(n + 1) * 1024],
            (((1,), (1,)), ((), ())),
            preferred_element_type=F32,
        ).astype(BF16)
        blocks = [flipped[:, k * BLK:(k + 1) * BLK] for k in range(8)]
        for k in range(8):
            self_t[n * 8 + k] = blocks[k]
        moved = jnp.dot(jnp.concatenate(blocks, axis=0), perm, preferred_element_type=F32)
        perm_t[n * 8:(n + 1) * 8] = moved.astype(BF16).reshape(8, BLK, BLK)
    loads[4].wait()
    for r in range(REL):
        for half in range(2):
            piece = weight_ref[r, :, half * BLK:(half + 1) * BLK]
            weight_t[half * BLK:(half + 1) * BLK, r * BLK:(r + 1) * BLK] = (
                piece.astype(F32).T.astype(BF16)
            )
    for load in loads[5:]:
        load.wait()

    def mix(b):
        own_rows = self_t[b].astype(F32)
        for r in range(REL):
            count = count_ref[r, b]
            tiles = []
            gathered = []
            degree = None
            for s in range(SLOTS):
                words = pattern_ref[b, r, s]
                if s > 0:
                    words = words & jnp.where(s < count, jnp.int32(65535), jnp.int32(0))
                bits = lax.population_count(words)
                degree = bits if degree is None else degree + bits
                for j in range(16):
                    tiles.append((words & (1 << j)).astype(F32))
                gathered.append(perm_t[source_ref[r, s, b]])
            adj = jnp.concatenate(tiles, axis=0).astype(BF16)
            sources = jnp.concatenate(gathered, axis=1)
            summed = jnp.dot(sources, adj, preferred_element_type=F32)
            total = 1.0 + jnp.sum(degree.astype(F32), axis=0, keepdims=True)
            mixed_t[b, r * BLK:(r + 1) * BLK, :] = ((own_rows + summed) * (1.0 / total)).astype(BF16)

    def pair_copy(step):
        return pltpu.make_async_remote_copy(
            src_ref=pair_out.at[step],
            dst_ref=pair_in.at[step],
            send_sem=pair_send.at[step],
            recv_sem=pair_recv.at[step],
            device_id=at_feat(partner),
            device_id_type=MESH,
        )

    def shift(n):
        return 2 + n - 3 * (n // 2) - 2 * (n // 3)

    def offset(step):
        group, k = step // 4, step % 4
        return shift(group), shift(k)

    def target(step):
        dy, dx = offset(step)
        return device_at(dy, dx)

    def x_copy(step, dx):
        return pltpu.make_async_remote_copy(
            src_ref=x_out.at[step],
            dst_ref=x_in.at[step],
            send_sem=x_send.at[step],
            recv_sem=x_recv.at[step],
            device_id=at_feat(device_at(0, dx)),
            device_id_type=MESH,
        )

    def y_copy(step, dy):
        return pltpu.make_async_remote_copy(
            src_ref=y_out.at[step],
            dst_ref=y_in.at[step],
            send_sem=y_send.at[step],
            recv_sem=y_recv.at[step],
            device_id=at_feat(device_at(dy, 0)),
            device_id_type=MESH,
        )

    def turn_copy(kind, slot, d):
        return pltpu.make_async_remote_copy(
            src_ref=turn_out.at[kind, slot],
            dst_ref=turn_in.at[kind, slot],
            send_sem=turn_send.at[kind, slot],
            recv_sem=turn_recv.at[kind, slot],
            device_id=at_feat(device_at(d, 0) if kind == 0 else device_at(0, d)),
            device_id_type=MESH,
        )

    def project(step):
        mine = target(step)
        other = mine + 1 - 2 * core
        mix(mine)
        mix(other)
        both = jnp.concatenate([mixed_t[mine], mixed_t[other]], axis=1)
        part = jnp.dot(weight_t[...], both, preferred_element_type=F32)
        own_part[step] = part[:, :BLK]
        pair_out[step] = part[:, BLK:].astype(BF16)
        pair_copy(step).start()

    def top_sum(step):
        return own_part[step, :BLK] + pair_in[step, :BLK].astype(F32)

    def low_sum(step):
        return own_part[step, BLK:] + pair_in[step, BLK:].astype(F32)

    def send_top(step, k):
        x_out[step] = top_sum(step).astype(BF16)
        x_copy(step, DXS[k]).start()

    def send_low(step, dy):
        y_out[step] = low_sum(step).astype(BF16)
        y_copy(step, dy).start()

    def row_sum(group, mine):
        for k in range(3):
            x_copy(4 * group + k, DXS[k]).wait_recv()
            mine = mine + x_in[4 * group + k].astype(F32)
        return mine

    def send_row(group, dy):
        turn_out[0, group] = row_sum(group, keep_top[group]).astype(BF16)
        turn_copy(0, group, dy).start()

    def column_sum(k, mine):
        for group in range(3):
            y_copy(4 * group + k, 1).wait_recv()
            mine = mine + y_in[4 * group + k].astype(F32)
        return mine

    pl.semaphore_wait(barrier, 1 + 6 + NZ - 1)
    project(0)
    project(1)

    def four(group, carry):
        dy = shift(group)
        for k in range(4):
            step = 4 * group + k
            project(step + 2)
            pair_copy(step).wait_recv()
            if k < 3:
                send_top(step, k)
            else:
                keep_top[group] = top_sum(step)
            send_low(step, dy)
            if k == 2:
                @pl.when(group > 0)
                def _():
                    send_row(group - 1, shift(group - 1))
        return carry

    lax.fori_loop(0, 3, four, 0)
    for k in range(4):
        step = 12 + k
        if k < 2:
            project(step + 2)
        pair_copy(step).wait_recv()
        if k < 3:
            send_top(step, k)
            turn_out[1, k] = column_sum(k, low_sum(step)).astype(BF16)
            turn_copy(1, k, DXS[k]).start()
        if k == 2:
            send_row(2, 1)
    top = row_sum(3, top_sum(15))
    low = column_sum(3, low_sum(15))
    for slot in range(3):
        turn_copy(0, slot, 1).wait_recv()
        top = top + turn_in[0, slot].astype(F32)
        turn_copy(1, slot, 1).wait_recv()
        low = low + turn_in[1, slot].astype(F32)

    types = jnp.broadcast_to(type_ref[...].astype(F32), (BLK, BLK)).T
    for half in range(2):
        cols = slice(half * BLK, (half + 1) * BLK)
        pre = (top, low)[half].T
        gains = gain_ref[:, cols]
        gain = jnp.where(types == 0.0, gains[0:1], jnp.where(types == 1.0, gains[1:2], gains[2:3]))
        sig = jax.nn.sigmoid(pre)
        act_ref[:, cols] = (pre * sig * gain).astype(BF16)
        slope = cot_ref[:, cols].astype(F32) * gain * (sig * (1.0 + pre * (1.0 - sig)))
        slope_all[half, me] = slope.astype(BF16)

    def to_core(half, block, slot):
        return pltpu.make_async_remote_copy(
            src_ref=slope_all.at[half, block],
            dst_ref=slope_all.at[half, block],
            send_sem=core_send.at[half, slot],
            recv_sem=core_recv.at[half, slot],
            device_id=at_feat(partner),
            device_id_type=MESH,
        )

    def over_x(half, block, line, dx):
        rows = pl.ds(64 if line > 0 else 0, 64)
        return pltpu.make_async_remote_copy(
            src_ref=slope_all.at[half, block, rows],
            dst_ref=slope_all.at[half, block, rows],
            send_sem=agx_send.at[half, line, dx],
            recv_sem=agx_recv.at[half, line, dx],
            device_id=at_feat(device_at(0, dx)),
            device_id_type=MESH,
        )

    def over_y(half, block, line, dy):
        rows = pl.ds(0 if line > 0 else 64, 64)
        return pltpu.make_async_remote_copy(
            src_ref=slope_all.at[half, block, rows],
            dst_ref=slope_all.at[half, block, rows],
            send_sem=agy_send.at[half, line, dy],
            recv_sem=agy_recv.at[half, line, dy],
            device_id=at_feat(device_at(dy, 0)),
            device_id_type=MESH,
        )

    for half in range(2):
        for line in range(2):
            for d in DXS[:3]:
                over_x(half, me, line, d).start()
                over_y(half, me, line, d).start()
        to_core(half, me, 0).start()

    def forward(half):
        for d in (1, 3, 2):
            across = device_at(0, 4 - d)
            over_x(half, across, 0, d).wait_recv()
            for e in DXS[:3]:
                over_y(half, across, 1 + d, e).start()
            down = device_at(4 - d, 0)
            over_y(half, down, 0, d).wait_recv()
            for e in DXS[:3]:
                over_x(half, down, 1 + d, e).start()

    def arrived(half, dy, dx):
        block = device_at(4 - dy, 4 - dx)
        if dx > 0:
            over_x(half, block, 1 + dy, dx).wait_recv()
        if dy > 0:
            over_y(half, block, 1 + dx, dy).wait_recv()
        return block

    order = [(0, 1), (0, 3), (1, 0), (3, 0), (0, 2), (2, 0), (1, 1), (1, 3), (3, 1), (3, 3),
             (1, 2), (2, 1), (3, 2), (2, 3), (2, 2)]

    def relay(half):
        for dy, dx in order:
            block = arrived(half, dy, dx)
            to_core(half, block, dy * 4 + dx).start()

    def gradient(half):
        places = [(0, 0)] + order
        for chunk in range(4):
            lhs, rhs = [], []
            for dy, dx in places[4 * chunk:4 * chunk + 4]:
                block = device_at((4 - dy) % 4, (4 - dx) % 4)
                twin = block + 1 - 2 * core
                to_core(half, twin, dy * 4 + dx).wait_recv()
                lhs += [mixed_t[block], mixed_t[twin]]
                rhs += [slope_all[half, block], slope_all[half, twin]]
            product = jnp.dot(
                jnp.concatenate(lhs, axis=1),
                jnp.concatenate(rhs, axis=0),
                preferred_element_type=F32,
            )
            if chunk == 0:
                grad_acc[...] = product
            else:
                grad_acc[...] += product

    def scatter(half, dz):
        return pltpu.make_async_remote_copy(
            src_ref=wg_out.at[half, (dom + dz) % NZ],
            dst_ref=wg_in.at[half, dz],
            send_sem=zs_send.at[half, dz],
            recv_sem=zs_recv.at[half, dz],
            device_id=((dom + dz) % NZ, me),
            device_id_type=MESH,
        )

    def spread(half, dz, part):
        return pltpu.make_async_remote_copy(
            src_ref=wg_all.at[half, part],
            dst_ref=wg_all.at[half, part],
            send_sem=zb_send.at[half, dz],
            recv_sem=zb_recv.at[half, dz],
            device_id=((dom + dz) % NZ, me),
            device_id_type=MESH,
        )

    zorder = (4, 3, 5, 2, 6, 1, 7)

    def scatter_all(half):
        for p in range(NZ):
            wg_out[half, p] = grad_acc[p * PART:(p + 1) * PART, :].astype(BF16)
        for dz in zorder:
            scatter(half, dz).start()
        return grad_acc[pl.ds(pl.multiple_of(dom * PART, 8), PART), :]

    def spread_all(half, own):
        for dz in reversed(zorder):
            scatter(half, dz).wait_recv()
            own = own + wg_in[half, dz].astype(F32)
        wg_all[half, dom] = own.astype(BF16)
        for dz in zorder:
            spread(half, dz, dom).start()

    forward(0)
    forward(1)
    relay(0)
    gradient(0)
    first = scatter_all(0)
    relay(1)
    gradient(1)
    second = scatter_all(1)
    spread_all(0, first)
    spread_all(1, second)

    def drain(step, carry):
        pair_copy(step).wait_send()
        return carry

    lax.fori_loop(0, 16, drain, 0)
    for step in range(16):
        if step % 4 < 3:
            x_copy(step, 1).wait_send()
        if step < 12:
            y_copy(step, 1).wait_send()
    for slot in range(3):
        turn_copy(0, slot, 1).wait_send()
        turn_copy(1, slot, 1).wait_send()
    for half in range(2):
        for d in range(1, 4):
            for line in range(5):
                over_x(half, me, line, d).wait_send()
                over_y(half, me, line, d).wait_send()
        for slot in range(16):
            to_core(half, me, slot).wait_send()
        for dz in range(1, NZ):
            scatter(half, dz).wait_send()
            spread(half, dz, dom).wait_send()
    for half in range(2):
        for dz in range(1, NZ):
            spread(half, dz, (dom + NZ - dz) % NZ).wait_recv()


def finish(act_in, wg_in, act_ref, grad_ref):
    act_ref[...] = act_in[...]
    for half in range(2):
        for p in range(NZ):
            grad_ref[p * PART:(p + 1) * PART, half * BLK:(half + 1) * BLK] = wg_in[half, p].astype(F32)


def body(
    features, proj_weight, source_block, slot_count, block_pattern, node_type, type_gain, cotangent
):
    vmem = pl.BlockSpec(memory_space=pltpu.VMEM)
    activations, parts = pl.pallas_call(
        kernel,
        out_shape=(
            jax.ShapeDtypeStruct((BLK, HID), BF16),
            jax.ShapeDtypeStruct((2, NZ, PART, BLK), BF16),
        ),
        in_specs=[pl.BlockSpec(memory_space=pl.ANY)] * 8,
        out_specs=(vmem, vmem),
        scratch_shapes=[
            pltpu.VMEM((PB * BLK, BLK), BF16),
            pltpu.VMEM((REL, BLK, HID), BF16),
            pltpu.SMEM((REL, SLOTS, PB), jnp.int32),
            pltpu.SMEM((REL, PB), jnp.int32),
            pltpu.VMEM((PB, REL, SLOTS, 8, BLK), jnp.int32),
            pltpu.VMEM((1, BLK), jnp.int32),
            pltpu.VMEM((NTYPES, HID), F32),
            pltpu.VMEM((BLK, HID), BF16),
            pltpu.SemaphoreType.DMA((11,)),
            pltpu.VMEM((PB, BLK, BLK), BF16),
            pltpu.VMEM((PB, BLK, BLK), BF16),
            pltpu.VMEM((HID, REL * BLK), BF16),
            pltpu.VMEM((PB, REL * BLK, BLK), BF16),
            pltpu.VMEM((16, HID, BLK), F32),
            pltpu.VMEM((3, BLK, BLK), F32),
            pltpu.VMEM((16, HID, BLK), BF16),
            pltpu.VMEM((16, HID, BLK), BF16),
            pltpu.VMEM((16, BLK, BLK), BF16),
            pltpu.VMEM((16, BLK, BLK), BF16),
            pltpu.VMEM((16, BLK, BLK), BF16),
            pltpu.VMEM((16, BLK, BLK), BF16),
            pltpu.VMEM((2, 3, BLK, BLK), BF16),
            pltpu.VMEM((2, 3, BLK, BLK), BF16),
            pltpu.VMEM((2, PB, BLK, BLK), BF16),
            pltpu.VMEM((REL * BLK, BLK), F32),
            pltpu.VMEM((2, NZ, PART, BLK), BF16),
            pltpu.VMEM((2, NZ, PART, BLK), BF16),
            pltpu.SemaphoreType.DMA((16,)),
            pltpu.SemaphoreType.DMA((16,)),
            pltpu.SemaphoreType.DMA((16,)),
            pltpu.SemaphoreType.DMA((16,)),
            pltpu.SemaphoreType.DMA((16,)),
            pltpu.SemaphoreType.DMA((16,)),
            pltpu.SemaphoreType.DMA((2, 3)),
            pltpu.SemaphoreType.DMA((2, 3)),
            pltpu.SemaphoreType.DMA((2, 5, 4)),
            pltpu.SemaphoreType.DMA((2, 5, 4)),
            pltpu.SemaphoreType.DMA((2, 5, 4)),
            pltpu.SemaphoreType.DMA((2, 5, 4)),
            pltpu.SemaphoreType.DMA((2, 16)),
            pltpu.SemaphoreType.DMA((2, 16)),
            pltpu.SemaphoreType.DMA((2, NZ)),
            pltpu.SemaphoreType.DMA((2, NZ)),
            pltpu.SemaphoreType.DMA((2, NZ)),
            pltpu.SemaphoreType.DMA((2, NZ)),
        ],
        compiler_params=pltpu.CompilerParams(
            collective_id=0, has_side_effects=True, vmem_limit_bytes=60 * 1024 * 1024
        ),
        name="graph_conv",
    )(
        features,
        proj_weight,
        jnp.transpose(source_block, (1, 2, 0)),
        jnp.transpose(slot_count, (1, 0)),
        block_pattern,
        node_type.reshape(1, BLK),
        type_gain,
        cotangent,
    )
    activations, grad = pl.pallas_call(
        finish,
        out_shape=(
            jax.ShapeDtypeStruct((BLK, HID), BF16),
            jax.ShapeDtypeStruct((REL * BLK, HID), F32),
        ),
        in_specs=[vmem, vmem],
        out_specs=(vmem, vmem),
        name="finish",
    )(activations, parts)
    return activations, grad.reshape(REL, BLK, HID)


def solution(mesh):
    placed = (
        P("dom", "feat"),
        P(None, "feat", None),
        P("dom", None, None),
        P("dom", None),
        P("dom", None, None, None, None),
        P(("dom", "feat")),
        P(),
        P(("dom", "feat"), None),
    )
    return jax.shard_map(
        body,
        mesh=mesh,
        in_specs=placed,
        out_specs=(P(("dom", "feat"), None), P(None, "feat", None)),
        check_vma=False,
    )
```

```python
import functools

import jax
import jax.numpy as jnp
from jax import lax
from jax.experimental import pallas as pl
from jax.experimental.pallas import tpu as pltpu
from jax.sharding import PartitionSpec as P

MESH = pl.DeviceIdType.MESH
F32 = jnp.float32
BF16 = jnp.bfloat16
BLK = 128
REL = 3
NTYPES = 3
SLOTS = 4
PB = 32
HID = 256
NZ = 8
DXS = (2, 3, 1, 0)
PART = REL * BLK // NZ


def kernel(
    feat_hbm,
    weight_hbm,
    source_hbm,
    count_hbm,
    pattern_hbm,
    type_hbm,
    gain_hbm,
    cot_hbm,
    act_ref,
    wg_all,
    feat_ref,
    weight_ref,
    source_ref,
    count_ref,
    pattern_ref,
    type_ref,
    gain_ref,
    cot_ref,
    load_sem,
    self_t,
    perm_t,
    weight_t,
    mixed_t,
    own_part,
    keep_top,
    pair_out,
    pair_in,
    x_out,
    x_in,
    y_out,
    y_in,
    turn_out,
    turn_in,
    slope_all,
    grad_acc,
    wg_out,
    wg_in,
    pair_send,
    pair_recv,
    x_send,
    x_recv,
    y_send,
    y_recv,
    turn_send,
    turn_recv,
    agx_send,
    agx_recv,
    agy_send,
    agy_recv,
    core_send,
    core_recv,
    zs_send,
    zs_recv,
    zb_send,
    zb_recv,
):
    dom = lax.axis_index("dom")
    me = lax.axis_index("feat")
    core = me % 2
    chip = me // 2
    x = chip % 4
    y = chip // 4
    partner = me + 1 - 2 * core

    def at_feat(dest):
        return (dom, dest)

    def device_at(dy, dx):
        return (((y + dy) % 4) * 4 + (x + dx) % 4) * 2 + core

    def piece_of(ref, n):
        return ref.at[pl.ds(n * 1024, 1024)]

    loads = [
        pltpu.make_async_copy(src, dst, load_sem.at[n])
        for n, (src, dst) in enumerate((
            (piece_of(feat_hbm, 0), piece_of(feat_ref, 0)),
            (piece_of(feat_hbm, 1), piece_of(feat_ref, 1)),
            (piece_of(feat_hbm, 2), piece_of(feat_ref, 2)),
            (piece_of(feat_hbm, 3), piece_of(feat_ref, 3)),
            (weight_hbm, weight_ref),
            (source_hbm, source_ref),
            (count_hbm, count_ref),
            (pattern_hbm, pattern_ref),
            (type_hbm, type_ref),
            (gain_hbm, gain_ref),
            (cot_hbm, cot_ref),
        ))
    ]
    for load in loads:
        load.start()

    barrier = pltpu.get_barrier_semaphore()

    def greet(dest):
        pl.semaphore_signal(barrier, inc=1, device_id=dest, device_id_type=MESH)

    greet(at_feat(partner))
    for d in range(1, 4):
        greet(at_feat(device_at(0, d)))
        greet(at_feat(device_at(d, 0)))
    for dz in range(1, NZ):
        greet(((dom + dz) % NZ, me))

    row = lax.broadcasted_iota(jnp.int32, (BLK, BLK), 0)
    col = lax.broadcasted_iota(jnp.int32, (BLK, BLK), 1)
    scale = 1.0 / (jnp.int32(1) << (col // 8)).astype(F32)
    perm = jnp.where(row == (col % 8) * 16 + col // 8, scale, 0.0).astype(BF16)
    eye = jnp.where(row == col, 1.0, 0.0).astype(BF16)

    for n in range(4):
        loads[n].wait()
        flipped = lax.dot_general(
            eye,
            feat_ref[n * 1024:(n + 1) * 1024],
            (((1,), (1,)), ((), ())),
            preferred_element_type=F32,
        ).astype(BF16)
        blocks = [flipped[:, k * BLK:(k + 1) * BLK] for k in range(8)]
        for k in range(8):
            self_t[n * 8 + k] = blocks[k]
        moved = jnp.dot(jnp.concatenate(blocks, axis=0), perm, preferred_element_type=F32)
        perm_t[n * 8:(n + 1) * 8] = moved.astype(BF16).reshape(8, BLK, BLK)
    loads[4].wait()
    for r in range(REL):
        for half in range(2):
            piece = weight_ref[r, :, half * BLK:(half + 1) * BLK]
            weight_t[half * BLK:(half + 1) * BLK, r * BLK:(r + 1) * BLK] = (
                piece.astype(F32).T.astype(BF16)
            )
    for load in loads[5:]:
        load.wait()

    def mix(b):
        own_rows = self_t[b].astype(F32)
        for r in range(REL):
            count = count_ref[r, b]
            tiles = []
            gathered = []
            degree = None
            for s in range(SLOTS):
                words = pattern_ref[b, r, s]
                if s > 0:
                    words = words & jnp.where(s < count, jnp.int32(65535), jnp.int32(0))
                bits = lax.population_count(words)
                degree = bits if degree is None else degree + bits
                for j in range(16):
                    tiles.append((words & (1 << j)).astype(F32))
                gathered.append(perm_t[source_ref[r, s, b]])
            adj = jnp.concatenate(tiles, axis=0).astype(BF16)
            sources = jnp.concatenate(gathered, axis=1)
            summed = jnp.dot(sources, adj, preferred_element_type=F32)
            total = 1.0 + jnp.sum(degree.astype(F32), axis=0, keepdims=True)
            mixed_t[b, r * BLK:(r + 1) * BLK, :] = ((own_rows + summed) * (1.0 / total)).astype(BF16)

    def pair_copy(step):
        return pltpu.make_async_remote_copy(
            src_ref=pair_out.at[step],
            dst_ref=pair_in.at[step],
            send_sem=pair_send.at[step],
            recv_sem=pair_recv.at[step],
            device_id=at_feat(partner),
            device_id_type=MESH,
        )

    def shift(n):
        return 2 + n - 3 * (n // 2) - 2 * (n // 3)

    def offset(step):
        group, k = step // 4, step % 4
        return shift(group), shift(k)

    def target(step):
        dy, dx = offset(step)
        return device_at(dy, dx)

    def x_copy(step, dx):
        return pltpu.make_async_remote_copy(
            src_ref=x_out.at[step],
            dst_ref=x_in.at[step],
            send_sem=x_send.at[step],
            recv_sem=x_recv.at[step],
            device_id=at_feat(device_at(0, dx)),
            device_id_type=MESH,
        )

    def y_copy(step, dy):
        return pltpu.make_async_remote_copy(
            src_ref=y_out.at[step],
            dst_ref=y_in.at[step],
            send_sem=y_send.at[step],
            recv_sem=y_recv.at[step],
            device_id=at_feat(device_at(dy, 0)),
            device_id_type=MESH,
        )

    def turn_copy(kind, slot, d):
        return pltpu.make_async_remote_copy(
            src_ref=turn_out.at[kind, slot],
            dst_ref=turn_in.at[kind, slot],
            send_sem=turn_send.at[kind, slot],
            recv_sem=turn_recv.at[kind, slot],
            device_id=at_feat(device_at(d, 0) if kind == 0 else device_at(0, d)),
            device_id_type=MESH,
        )

    def mix_both(step):
        mine = target(step)
        mix(mine)
        mix(mine + 1 - 2 * core)

    def project(step):
        mine = target(step)
        other = mine + 1 - 2 * core
        both = jnp.concatenate([mixed_t[mine], mixed_t[other]], axis=1)
        part = jnp.dot(weight_t[...], both, preferred_element_type=F32)
        own_part[step] = part[:, :BLK]
        pair_out[step] = part[:, BLK:].astype(BF16)

    def top_sum(step):
        return own_part[step, :BLK] + pair_in[step, :BLK].astype(F32)

    def low_sum(step):
        return own_part[step, BLK:] + pair_in[step, BLK:].astype(F32)

    def send_top(step, k):
        x_out[step] = top_sum(step).astype(BF16)
        x_copy(step, DXS[k]).start()

    def send_low(step, dy):
        y_out[step] = low_sum(step).astype(BF16)
        y_copy(step, dy).start()

    def row_sum(group, mine):
        for k in range(3):
            x_copy(4 * group + k, DXS[k]).wait_recv()
            mine = mine + x_in[4 * group + k].astype(F32)
        return mine

    def send_row(group, dy):
        turn_out[0, group] = row_sum(group, keep_top[group]).astype(BF16)
        turn_copy(0, group, dy).start()

    def column_sum(k, mine):
        for group in range(3):
            y_copy(4 * group + k, 1).wait_recv()
            mine = mine + y_in[4 * group + k].astype(F32)
        return mine

    pl.semaphore_wait(barrier, 1 + 6 + NZ - 1)
    mix_both(0)
    project(0)
    mix_both(1)
    pair_copy(0).start()
    project(1)
    mix_both(2)
    pair_copy(1).start()

    def four(group, carry):
        dy = shift(group)
        for k in range(4):
            step = 4 * group + k
            project(step + 2)
            mix_both(step + 3)
            pair_copy(step + 2).start()
            pair_copy(step).wait_recv()
            if k < 3:
                send_top(step, k)
            else:
                keep_top[group] = top_sum(step)
            send_low(step, dy)
            if k == 2:
                @pl.when(group > 0)
                def _():
                    send_row(group - 1, shift(group - 1))
        return carry

    lax.fori_loop(0, 3, four, 0)
    for k in range(4):
        step = 12 + k
        if k < 2:
            project(step + 2)
            if k < 1:
                mix_both(step + 3)
            pair_copy(step + 2).start()
        pair_copy(step).wait_recv()
        if k < 3:
            send_top(step, k)
            turn_out[1, k] = column_sum(k, low_sum(step)).astype(BF16)
            turn_copy(1, k, DXS[k]).start()
        if k == 2:
            send_row(2, 1)
    def to_core(half, block, slot):
        return pltpu.make_async_remote_copy(
            src_ref=slope_all.at[half, block],
            dst_ref=slope_all.at[half, block],
            send_sem=core_send.at[half, slot],
            recv_sem=core_recv.at[half, slot],
            device_id=at_feat(partner),
            device_id_type=MESH,
        )

    def over_x(half, block, line, dx):
        rows = pl.ds(64 if line > 0 else 0, 64)
        return pltpu.make_async_remote_copy(
            src_ref=slope_all.at[half, block, rows],
            dst_ref=slope_all.at[half, block, rows],
            send_sem=agx_send.at[half, line, dx],
            recv_sem=agx_recv.at[half, line, dx],
            device_id=at_feat(device_at(0, dx)),
            device_id_type=MESH,
        )

    def over_y(half, block, line, dy):
        rows = pl.ds(0 if line > 0 else 64, 64)
        return pltpu.make_async_remote_copy(
            src_ref=slope_all.at[half, block, rows],
            dst_ref=slope_all.at[half, block, rows],
            send_sem=agy_send.at[half, line, dy],
            recv_sem=agy_recv.at[half, line, dy],
            device_id=at_feat(device_at(dy, 0)),
            device_id_type=MESH,
        )

    types = jnp.broadcast_to(type_ref[...].astype(F32), (BLK, BLK)).T
    for half in range(2):
        total = row_sum(3, top_sum(15)) if half == 0 else column_sum(3, low_sum(15))
        for slot in range(3):
            turn_copy(half, slot, 1).wait_recv()
            total = total + turn_in[half, slot].astype(F32)
        cols = slice(half * BLK, (half + 1) * BLK)
        pre = total.T
        gains = gain_ref[:, cols]
        gain = jnp.where(types == 0.0, gains[0:1], jnp.where(types == 1.0, gains[1:2], gains[2:3]))
        sig = jax.nn.sigmoid(pre)
        slope = cot_ref[:, cols].astype(F32) * gain * (sig * (1.0 + pre * (1.0 - sig)))
        slope_all[half, me] = slope.astype(BF16)
        act_ref[:, cols] = (pre * sig * gain).astype(BF16)
        for line in range(2):
            for d in DXS[:3]:
                over_x(half, me, line, d).start()
                over_y(half, me, line, d).start()
        to_core(half, me, 0).start()

    def forward(half):
        for d in (1, 3, 2):
            across = device_at(0, 4 - d)
            over_x(half, across, 0, d).wait_recv()
            for e in DXS[:3]:
                over_y(half, across, 1 + d, e).start()
            down = device_at(4 - d, 0)
            over_y(half, down, 0, d).wait_recv()
            for e in DXS[:3]:
                over_x(half, down, 1 + d, e).start()

    def arrived(half, dy, dx):
        block = device_at(4 - dy, 4 - dx)
        if dx > 0:
            over_x(half, block, 1 + dy, dx).wait_recv()
        if dy > 0:
            over_y(half, block, 1 + dx, dy).wait_recv()
        return block

    order = [(0, 1), (0, 3), (1, 0), (3, 0), (0, 2), (2, 0), (1, 1), (1, 3), (3, 1), (3, 3),
             (1, 2), (2, 1), (3, 2), (2, 3), (2, 2)]

    def relay(half):
        for dy, dx in order:
            block = arrived(half, dy, dx)
            to_core(half, block, dy * 4 + dx).start()

    def gradient(half):
        places = [(0, 0)] + order
        for chunk in range(4):
            lhs, rhs = [], []
            for dy, dx in places[4 * chunk:4 * chunk + 4]:
                block = device_at((4 - dy) % 4, (4 - dx) % 4)
                twin = block + 1 - 2 * core
                to_core(half, twin, dy * 4 + dx).wait_recv()
                lhs += [mixed_t[block], mixed_t[twin]]
                rhs += [slope_all[half, block], slope_all[half, twin]]
            product = jnp.dot(
                jnp.concatenate(lhs, axis=1),
                jnp.concatenate(rhs, axis=0),
                preferred_element_type=F32,
            )
            if chunk == 0:
                grad_acc[...] = product
            else:
                grad_acc[...] += product

    def scatter(half, dz):
        return pltpu.make_async_remote_copy(
            src_ref=wg_out.at[half, (dom + dz) % NZ],
            dst_ref=wg_in.at[half, dz],
            send_sem=zs_send.at[half, dz],
            recv_sem=zs_recv.at[half, dz],
            device_id=((dom + dz) % NZ, me),
            device_id_type=MESH,
        )

    def spread(half, dz, part):
        return pltpu.make_async_remote_copy(
            src_ref=wg_all.at[half, part],
            dst_ref=wg_all.at[half, part],
            send_sem=zb_send.at[half, dz],
            recv_sem=zb_recv.at[half, dz],
            device_id=((dom + dz) % NZ, me),
            device_id_type=MESH,
        )

    zorder = (4, 3, 5, 2, 6, 1, 7)

    def scatter_all(half):
        for p in range(NZ):
            wg_out[half, p] = grad_acc[p * PART:(p + 1) * PART, :].astype(BF16)
        for dz in zorder:
            scatter(half, dz).start()
        return grad_acc[pl.ds(pl.multiple_of(dom * PART, 8), PART), :]

    def spread_all(half, own):
        for dz in reversed(zorder):
            scatter(half, dz).wait_recv()
            own = own + wg_in[half, dz].astype(F32)
        wg_all[half, dom] = own.astype(BF16)
        for dz in zorder:
            spread(half, dz, dom).start()

    forward(0)
    forward(1)
    relay(0)
    gradient(0)
    first = scatter_all(0)
    relay(1)
    gradient(1)
    second = scatter_all(1)
    spread_all(0, first)
    spread_all(1, second)

    def drain(step, carry):
        pair_copy(step).wait_send()
        return carry

    lax.fori_loop(0, 16, drain, 0)
    for step in range(16):
        if step % 4 < 3:
            x_copy(step, 1).wait_send()
        if step < 12:
            y_copy(step, 1).wait_send()
    for slot in range(3):
        turn_copy(0, slot, 1).wait_send()
        turn_copy(1, slot, 1).wait_send()
    for half in range(2):
        for d in range(1, 4):
            for line in range(5):
                over_x(half, me, line, d).wait_send()
                over_y(half, me, line, d).wait_send()
        for slot in range(16):
            to_core(half, me, slot).wait_send()
        for dz in range(1, NZ):
            scatter(half, dz).wait_send()
            spread(half, dz, dom).wait_send()
    for half in range(2):
        for dz in range(1, NZ):
            spread(half, dz, (dom + NZ - dz) % NZ).wait_recv()


def finish(act_in, wg_in, act_ref, grad_ref):
    act_ref[...] = act_in[...]
    for half in range(2):
        for p in range(NZ):
            grad_ref[p * PART:(p + 1) * PART, half * BLK:(half + 1) * BLK] = wg_in[half, p].astype(F32)


def body(
    features, proj_weight, source_block, slot_count, block_pattern, node_type, type_gain, cotangent
):
    vmem = pl.BlockSpec(memory_space=pltpu.VMEM)
    activations, parts = pl.pallas_call(
        kernel,
        out_shape=(
            jax.ShapeDtypeStruct((BLK, HID), BF16),
            jax.ShapeDtypeStruct((2, NZ, PART, BLK), BF16),
        ),
        in_specs=[pl.BlockSpec(memory_space=pl.ANY)] * 8,
        out_specs=(vmem, vmem),
        scratch_shapes=[
            pltpu.VMEM((PB * BLK, BLK), BF16),
            pltpu.VMEM((REL, BLK, HID), BF16),
            pltpu.SMEM((REL, SLOTS, PB), jnp.int32),
            pltpu.SMEM((REL, PB), jnp.int32),
            pltpu.VMEM((PB, REL, SLOTS, 8, BLK), jnp.int32),
            pltpu.VMEM((1, BLK), jnp.int32),
            pltpu.VMEM((NTYPES, HID), F32),
            pltpu.VMEM((BLK, HID), BF16),
            pltpu.SemaphoreType.DMA((11,)),
            pltpu.VMEM((PB, BLK, BLK), BF16),
            pltpu.VMEM((PB, BLK, BLK), BF16),
            pltpu.VMEM((HID, REL * BLK), BF16),
            pltpu.VMEM((PB, REL * BLK, BLK), BF16),
            pltpu.VMEM((16, HID, BLK), F32),
            pltpu.VMEM((3, BLK, BLK), F32),
            pltpu.VMEM((16, HID, BLK), BF16),
            pltpu.VMEM((16, HID, BLK), BF16),
            pltpu.VMEM((16, BLK, BLK), BF16),
            pltpu.VMEM((16, BLK, BLK), BF16),
            pltpu.VMEM((16, BLK, BLK), BF16),
            pltpu.VMEM((16, BLK, BLK), BF16),
            pltpu.VMEM((2, 3, BLK, BLK), BF16),
            pltpu.VMEM((2, 3, BLK, BLK), BF16),
            pltpu.VMEM((2, PB, BLK, BLK), BF16),
            pltpu.VMEM((REL * BLK, BLK), F32),
            pltpu.VMEM((2, NZ, PART, BLK), BF16),
            pltpu.VMEM((2, NZ, PART, BLK), BF16),
            pltpu.SemaphoreType.DMA((16,)),
            pltpu.SemaphoreType.DMA((16,)),
            pltpu.SemaphoreType.DMA((16,)),
            pltpu.SemaphoreType.DMA((16,)),
            pltpu.SemaphoreType.DMA((16,)),
            pltpu.SemaphoreType.DMA((16,)),
            pltpu.SemaphoreType.DMA((2, 3)),
            pltpu.SemaphoreType.DMA((2, 3)),
            pltpu.SemaphoreType.DMA((2, 5, 4)),
            pltpu.SemaphoreType.DMA((2, 5, 4)),
            pltpu.SemaphoreType.DMA((2, 5, 4)),
            pltpu.SemaphoreType.DMA((2, 5, 4)),
            pltpu.SemaphoreType.DMA((2, 16)),
            pltpu.SemaphoreType.DMA((2, 16)),
            pltpu.SemaphoreType.DMA((2, NZ)),
            pltpu.SemaphoreType.DMA((2, NZ)),
            pltpu.SemaphoreType.DMA((2, NZ)),
            pltpu.SemaphoreType.DMA((2, NZ)),
        ],
        compiler_params=pltpu.CompilerParams(
            collective_id=0, has_side_effects=True, vmem_limit_bytes=60 * 1024 * 1024
        ),
        name="graph_conv",
    )(
        features,
        proj_weight,
        jnp.transpose(source_block, (1, 2, 0)),
        jnp.transpose(slot_count, (1, 0)),
        block_pattern,
        node_type.reshape(1, BLK),
        type_gain,
        cotangent,
    )
    activations, grad = pl.pallas_call(
        finish,
        out_shape=(
            jax.ShapeDtypeStruct((BLK, HID), BF16),
            jax.ShapeDtypeStruct((REL * BLK, HID), F32),
        ),
        in_specs=[vmem, vmem],
        out_specs=(vmem, vmem),
        name="finish",
    )(activations, parts)
    return activations, grad.reshape(REL, BLK, HID)


def solution(mesh):
    placed = (
        P("dom", "feat"),
        P(None, "feat", None),
        P("dom", None, None),
        P("dom", None),
        P("dom", None, None, None, None),
        P(("dom", "feat")),
        P(),
        P(("dom", "feat"), None),
    )
    return jax.shard_map(
        body,
        mesh=mesh,
        in_specs=placed,
        out_specs=(P(("dom", "feat"), None), P(None, "feat", None)),
        check_vma=False,
    )
```

```python
import functools

import jax
import jax.numpy as jnp
from jax import lax
from jax.experimental import pallas as pl
from jax.experimental.pallas import tpu as pltpu
from jax.sharding import PartitionSpec as P

MESH = pl.DeviceIdType.MESH
F32 = jnp.float32
BF16 = jnp.bfloat16
BLK = 128
REL = 3
NTYPES = 3
SLOTS = 4
PB = 32
HID = 256
NZ = 8
DXS = (2, 3, 1, 0)
PART = REL * BLK // NZ


def kernel(
    feat_hbm,
    weight_hbm,
    source_hbm,
    count_hbm,
    pattern_hbm,
    type_hbm,
    gain_hbm,
    cot_hbm,
    act_ref,
    wg_all,
    feat_ref,
    weight_ref,
    source_ref,
    count_ref,
    pattern_ref,
    type_ref,
    gain_ref,
    cot_ref,
    load_sem,
    self_t,
    perm_t,
    weight_t,
    mixed_t,
    own_part,
    keep_top,
    pair_out,
    pair_in,
    x_out,
    x_in,
    y_out,
    y_in,
    turn_out,
    turn_in,
    slope_all,
    grad_acc,
    wg_out,
    wg_in,
    pair_send,
    pair_recv,
    x_send,
    x_recv,
    y_send,
    y_recv,
    turn_send,
    turn_recv,
    agx_send,
    agx_recv,
    agy_send,
    agy_recv,
    core_send,
    core_recv,
    zs_send,
    zs_recv,
    zb_send,
    zb_recv,
):
    dom = lax.axis_index("dom")
    me = lax.axis_index("feat")
    core = me % 2
    chip = me // 2
    x = chip % 4
    y = chip // 4
    partner = me + 1 - 2 * core

    def at_feat(dest):
        return (dom, dest)

    def device_at(dy, dx):
        return (((y + dy) % 4) * 4 + (x + dx) % 4) * 2 + core

    def piece_of(ref, n):
        return ref.at[pl.ds(n * 1024, 1024)]

    loads = [
        pltpu.make_async_copy(src, dst, load_sem.at[n])
        for n, (src, dst) in enumerate((
            (piece_of(feat_hbm, 0), piece_of(feat_ref, 0)),
            (piece_of(feat_hbm, 1), piece_of(feat_ref, 1)),
            (piece_of(feat_hbm, 2), piece_of(feat_ref, 2)),
            (piece_of(feat_hbm, 3), piece_of(feat_ref, 3)),
            (weight_hbm, weight_ref),
            (source_hbm, source_ref),
            (count_hbm, count_ref),
            (pattern_hbm, pattern_ref),
            (type_hbm, type_ref),
            (gain_hbm, gain_ref),
            (cot_hbm, cot_ref),
        ))
    ]
    for load in loads:
        load.start()

    barrier = pltpu.get_barrier_semaphore()

    def greet(dest):
        pl.semaphore_signal(barrier, inc=1, device_id=dest, device_id_type=MESH)

    greet(at_feat(partner))
    for d in range(1, 4):
        greet(at_feat(device_at(0, d)))
        greet(at_feat(device_at(d, 0)))
    for dz in range(1, NZ):
        greet(((dom + dz) % NZ, me))

    row = lax.broadcasted_iota(jnp.int32, (BLK, BLK), 0)
    col = lax.broadcasted_iota(jnp.int32, (BLK, BLK), 1)
    scale = 1.0 / (jnp.int32(1) << (col // 8)).astype(F32)
    perm = jnp.where(row == (col % 8) * 16 + col // 8, scale, 0.0).astype(BF16)
    eye = jnp.where(row == col, 1.0, 0.0).astype(BF16)

    for n in range(4):
        loads[n].wait()
        flipped = lax.dot_general(
            eye,
            feat_ref[n * 1024:(n + 1) * 1024],
            (((1,), (1,)), ((), ())),
            preferred_element_type=F32,
        ).astype(BF16)
        blocks = [flipped[:, k * BLK:(k + 1) * BLK] for k in range(8)]
        for k in range(8):
            self_t[n * 8 + k] = blocks[k]
        moved = jnp.dot(jnp.concatenate(blocks, axis=0), perm, preferred_element_type=F32)
        perm_t[n * 8:(n + 1) * 8] = moved.astype(BF16).reshape(8, BLK, BLK)
    loads[4].wait()
    for r in range(REL):
        for half in range(2):
            piece = weight_ref[r, :, half * BLK:(half + 1) * BLK]
            weight_t[half * BLK:(half + 1) * BLK, r * BLK:(r + 1) * BLK] = (
                piece.astype(F32).T.astype(BF16)
            )
    for load in loads[5:]:
        load.wait()

    def mix(b):
        own_rows = self_t[b].astype(F32)
        for r in range(REL):
            count = count_ref[r, b]
            tiles = []
            gathered = []
            degree = None
            for s in range(SLOTS):
                words = pattern_ref[b, r, s]
                if s > 0:
                    words = words & jnp.where(s < count, jnp.int32(65535), jnp.int32(0))
                bits = lax.population_count(words)
                degree = bits if degree is None else degree + bits
                for j in range(16):
                    tiles.append((words & (1 << j)).astype(F32))
                gathered.append(perm_t[source_ref[r, s, b]])
            adj = jnp.concatenate(tiles, axis=0).astype(BF16)
            sources = jnp.concatenate(gathered, axis=1)
            summed = jnp.dot(sources, adj, preferred_element_type=F32)
            total = 1.0 + jnp.sum(degree.astype(F32), axis=0, keepdims=True)
            mixed_t[b, r * BLK:(r + 1) * BLK, :] = ((own_rows + summed) * (1.0 / total)).astype(BF16)

    def pair_copy(step):
        return pltpu.make_async_remote_copy(
            src_ref=pair_out.at[step],
            dst_ref=pair_in.at[step],
            send_sem=pair_send.at[step],
            recv_sem=pair_recv.at[step],
            device_id=at_feat(partner),
            device_id_type=MESH,
        )

    def shift(n):
        return 2 + n - 3 * (n // 2) - 2 * (n // 3)

    def offset(step):
        group, k = step // 4, step % 4
        return shift(group), shift(k)

    def target(step):
        dy, dx = offset(step)
        return device_at(dy, dx)

    def x_copy(step, dx):
        return pltpu.make_async_remote_copy(
            src_ref=x_out.at[step],
            dst_ref=x_in.at[step],
            send_sem=x_send.at[step],
            recv_sem=x_recv.at[step],
            device_id=at_feat(device_at(0, dx)),
            device_id_type=MESH,
        )

    def y_copy(step, dy):
        return pltpu.make_async_remote_copy(
            src_ref=y_out.at[step],
            dst_ref=y_in.at[step],
            send_sem=y_send.at[step],
            recv_sem=y_recv.at[step],
            device_id=at_feat(device_at(dy, 0)),
            device_id_type=MESH,
        )

    def turn_copy(kind, slot, d):
        return pltpu.make_async_remote_copy(
            src_ref=turn_out.at[kind, slot],
            dst_ref=turn_in.at[kind, slot],
            send_sem=turn_send.at[kind, slot],
            recv_sem=turn_recv.at[kind, slot],
            device_id=at_feat(device_at(d, 0) if kind == 0 else device_at(0, d)),
            device_id_type=MESH,
        )

    def mix_both(step):
        mine = target(step)
        mix(mine)
        mix(mine + 1 - 2 * core)

    def project(step):
        mine = target(step)
        other = mine + 1 - 2 * core
        both = jnp.concatenate([mixed_t[mine], mixed_t[other]], axis=1)
        part = jnp.dot(weight_t[...], both, preferred_element_type=F32)
        own_part[step] = part[:, :BLK]
        pair_out[step] = part[:, BLK:].astype(BF16)

    def top_sum(step):
        return own_part[step, :BLK] + pair_in[step, :BLK].astype(F32)

    def low_sum(step):
        return own_part[step, BLK:] + pair_in[step, BLK:].astype(F32)

    def send_top(step, k):
        x_out[step] = top_sum(step).astype(BF16)
        x_copy(step, DXS[k]).start()

    def send_low(step, dy):
        y_out[step] = low_sum(step).astype(BF16)
        y_copy(step, dy).start()

    def row_sum(group, mine):
        for k in range(3):
            x_copy(4 * group + k, DXS[k]).wait_recv()
            mine = mine + x_in[4 * group + k].astype(F32)
        return mine

    def send_row(group, dy):
        turn_out[0, group] = row_sum(group, keep_top[group]).astype(BF16)
        turn_copy(0, group, dy).start()

    def column_sum(k, mine):
        for group in range(3):
            y_copy(4 * group + k, 1).wait_recv()
            mine = mine + y_in[4 * group + k].astype(F32)
        return mine

    pl.semaphore_wait(barrier, 1 + 6 + NZ - 1)
    mix_both(0)
    project(0)
    mix_both(1)
    pair_copy(0).start()
    project(1)
    mix_both(2)
    pair_copy(1).start()

    def four(group, carry):
        dy = shift(group)
        for k in range(4):
            step = 4 * group + k
            project(step + 2)
            mix_both(step + 3)
            pair_copy(step + 2).start()
            pair_copy(step).wait_recv()
            if k < 3:
                send_top(step, k)
            else:
                keep_top[group] = top_sum(step)
            send_low(step, dy)
            if k == 2:
                @pl.when(group > 0)
                def _():
                    send_row(group - 1, shift(group - 1))
        return carry

    lax.fori_loop(0, 3, four, 0)
    for k in range(4):
        step = 12 + k
        if k < 2:
            project(step + 2)
            if k < 1:
                mix_both(step + 3)
            pair_copy(step + 2).start()
        pair_copy(step).wait_recv()
        if k < 3:
            send_top(step, k)
            turn_out[1, k] = column_sum(k, low_sum(step)).astype(BF16)
            turn_copy(1, k, DXS[k]).start()
        if k == 2:
            send_row(2, 1)
    def to_core(half, block, slot):
        return pltpu.make_async_remote_copy(
            src_ref=slope_all.at[half, block],
            dst_ref=slope_all.at[half, block],
            send_sem=core_send.at[half, slot],
            recv_sem=core_recv.at[half, slot],
            device_id=at_feat(partner),
            device_id_type=MESH,
        )

    def over_x(half, block, line, dx):
        rows = pl.ds(64 if line > 0 else 0, 64)
        return pltpu.make_async_remote_copy(
            src_ref=slope_all.at[half, block, rows],
            dst_ref=slope_all.at[half, block, rows],
            send_sem=agx_send.at[half, line, dx],
            recv_sem=agx_recv.at[half, line, dx],
            device_id=at_feat(device_at(0, dx)),
            device_id_type=MESH,
        )

    def over_y(half, block, line, dy):
        rows = pl.ds(0 if line > 0 else 64, 64)
        return pltpu.make_async_remote_copy(
            src_ref=slope_all.at[half, block, rows],
            dst_ref=slope_all.at[half, block, rows],
            send_sem=agy_send.at[half, line, dy],
            recv_sem=agy_recv.at[half, line, dy],
            device_id=at_feat(device_at(dy, 0)),
            device_id_type=MESH,
        )

    types = jnp.broadcast_to(type_ref[...].astype(F32), (BLK, BLK)).T
    for half in range(2):
        total = row_sum(3, top_sum(15)) if half == 0 else column_sum(3, low_sum(15))
        for slot in range(3):
            turn_copy(half, slot, 1).wait_recv()
            total = total + turn_in[half, slot].astype(F32)
        cols = slice(half * BLK, (half + 1) * BLK)
        pre = total.T
        gains = gain_ref[:, cols]
        gain = jnp.where(types == 0.0, gains[0:1], jnp.where(types == 1.0, gains[1:2], gains[2:3]))
        sig = jax.nn.sigmoid(pre)
        slope = cot_ref[:, cols].astype(F32) * gain * (sig * (1.0 + pre * (1.0 - sig)))
        slope_all[half, me] = slope.astype(BF16)
        act_ref[:, cols] = (pre * sig * gain).astype(BF16)
        for line in range(2):
            for d in DXS[:3]:
                over_x(half, me, line, d).start()
                over_y(half, me, line, d).start()
        to_core(half, me, 0).start()

    def forward(half):
        for d in (1, 3, 2):
            across = device_at(0, 4 - d)
            over_x(half, across, 0, d).wait_recv()
            for e in DXS[:3]:
                over_y(half, across, 1 + d, e).start()
            down = device_at(4 - d, 0)
            over_y(half, down, 0, d).wait_recv()
            for e in DXS[:3]:
                over_x(half, down, 1 + d, e).start()

    def arrived(half, dy, dx):
        block = device_at(4 - dy, 4 - dx)
        if dx > 0:
            over_x(half, block, 1 + dy, dx).wait_recv()
        if dy > 0:
            over_y(half, block, 1 + dx, dy).wait_recv()
        return block

    order = [(0, 1), (0, 3), (1, 0), (3, 0), (0, 2), (2, 0), (1, 1), (1, 3), (3, 1), (3, 3),
             (1, 2), (2, 1), (3, 2), (2, 3), (2, 2)]

    def relay(half):
        for dy, dx in order:
            block = arrived(half, dy, dx)
            to_core(half, block, dy * 4 + dx).start()

    def gradient(half):
        places = [(0, 0)] + order
        for chunk in range(4):
            lhs, rhs = [], []
            for dy, dx in places[4 * chunk:4 * chunk + 4]:
                block = device_at((4 - dy) % 4, (4 - dx) % 4)
                twin = block + 1 - 2 * core
                to_core(half, twin, dy * 4 + dx).wait_recv()
                lhs += [mixed_t[block], mixed_t[twin]]
                rhs += [slope_all[half, block], slope_all[half, twin]]
            product = jnp.dot(
                jnp.concatenate(lhs, axis=1),
                jnp.concatenate(rhs, axis=0),
                preferred_element_type=F32,
            )
            if chunk == 0:
                grad_acc[...] = product
            else:
                grad_acc[...] += product

    def scatter(half, dz):
        return pltpu.make_async_remote_copy(
            src_ref=wg_out.at[half, (dom + dz) % NZ],
            dst_ref=wg_in.at[half, dz],
            send_sem=zs_send.at[half, dz],
            recv_sem=zs_recv.at[half, dz],
            device_id=((dom + dz) % NZ, me),
            device_id_type=MESH,
        )

    def spread(half, dz, part):
        return pltpu.make_async_remote_copy(
            src_ref=wg_all.at[half, part],
            dst_ref=wg_all.at[half, part],
            send_sem=zb_send.at[half, dz],
            recv_sem=zb_recv.at[half, dz],
            device_id=((dom + dz) % NZ, me),
            device_id_type=MESH,
        )

    zorder = (4, 3, 5, 2, 6, 1, 7)

    def scatter_all(half):
        for p in range(NZ):
            wg_out[half, p] = grad_acc[p * PART:(p + 1) * PART, :].astype(BF16)
        for dz in zorder:
            scatter(half, dz).start()
        return grad_acc[pl.ds(pl.multiple_of(dom * PART, 8), PART), :]

    def spread_all(half, own):
        for dz in reversed(zorder):
            scatter(half, dz).wait_recv()
            own = own + wg_in[half, dz].astype(F32)
        wg_all[half, dom] = own.astype(BF16)
        for dz in zorder:
            spread(half, dz, dom).start()

    forward(0)
    forward(1)
    relay(0)
    gradient(0)
    first = scatter_all(0)
    relay(1)
    gradient(1)
    second = scatter_all(1)
    spread_all(0, first)
    spread_all(1, second)

    def drain(step, carry):
        pair_copy(step).wait_send()
        return carry

    lax.fori_loop(0, 16, drain, 0)
    for step in range(16):
        if step % 4 < 3:
            x_copy(step, 1).wait_send()
        if step < 12:
            y_copy(step, 1).wait_send()
    for slot in range(3):
        turn_copy(0, slot, 1).wait_send()
        turn_copy(1, slot, 1).wait_send()
    for half in range(2):
        for d in range(1, 4):
            for line in range(5):
                over_x(half, me, line, d).wait_send()
                over_y(half, me, line, d).wait_send()
        for slot in range(16):
            to_core(half, me, slot).wait_send()
        for dz in range(1, NZ):
            scatter(half, dz).wait_send()
            spread(half, dz, dom).wait_send()
    for half in range(2):
        for dz in range(1, NZ):
            spread(half, dz, (dom + NZ - dz) % NZ).wait_recv()


def finish(act_in, wg_in, act_ref, grad_ref):
    act_ref[...] = act_in[...]
    for half in range(2):
        for p in range(NZ):
            grad_ref[p * PART:(p + 1) * PART, half * BLK:(half + 1) * BLK] = wg_in[half, p].astype(F32)


def body(
    features, proj_weight, source_block, slot_count, block_pattern, node_type, type_gain, cotangent
):
    vmem = pl.BlockSpec(memory_space=pltpu.VMEM)
    activations, parts = pl.pallas_call(
        kernel,
        out_shape=(
            jax.ShapeDtypeStruct((BLK, HID), BF16),
            jax.ShapeDtypeStruct((2, NZ, PART, BLK), BF16),
        ),
        in_specs=[pl.BlockSpec(memory_space=pltpu.HBM)] * 8,
        out_specs=(vmem, vmem),
        scratch_shapes=[
            pltpu.VMEM((PB * BLK, BLK), BF16),
            pltpu.VMEM((REL, BLK, HID), BF16),
            pltpu.SMEM((REL, SLOTS, PB), jnp.int32),
            pltpu.SMEM((REL, PB), jnp.int32),
            pltpu.VMEM((PB, REL, SLOTS, 8, BLK), jnp.int32),
            pltpu.VMEM((1, BLK), jnp.int32),
            pltpu.VMEM((NTYPES, HID), F32),
            pltpu.VMEM((BLK, HID), BF16),
            pltpu.SemaphoreType.DMA((11,)),
            pltpu.VMEM((PB, BLK, BLK), BF16),
            pltpu.VMEM((PB, BLK, BLK), BF16),
            pltpu.VMEM((HID, REL * BLK), BF16),
            pltpu.VMEM((PB, REL * BLK, BLK), BF16),
            pltpu.VMEM((16, HID, BLK), F32),
            pltpu.VMEM((3, BLK, BLK), F32),
            pltpu.VMEM((16, HID, BLK), BF16),
            pltpu.VMEM((16, HID, BLK), BF16),
            pltpu.VMEM((16, BLK, BLK), BF16),
            pltpu.VMEM((16, BLK, BLK), BF16),
            pltpu.VMEM((16, BLK, BLK), BF16),
            pltpu.VMEM((16, BLK, BLK), BF16),
            pltpu.VMEM((2, 3, BLK, BLK), BF16),
            pltpu.VMEM((2, 3, BLK, BLK), BF16),
            pltpu.VMEM((2, PB, BLK, BLK), BF16),
            pltpu.VMEM((REL * BLK, BLK), F32),
            pltpu.VMEM((2, NZ, PART, BLK), BF16),
            pltpu.VMEM((2, NZ, PART, BLK), BF16),
            pltpu.SemaphoreType.DMA((16,)),
            pltpu.SemaphoreType.DMA((16,)),
            pltpu.SemaphoreType.DMA((16,)),
            pltpu.SemaphoreType.DMA((16,)),
            pltpu.SemaphoreType.DMA((16,)),
            pltpu.SemaphoreType.DMA((16,)),
            pltpu.SemaphoreType.DMA((2, 3)),
            pltpu.SemaphoreType.DMA((2, 3)),
            pltpu.SemaphoreType.DMA((2, 5, 4)),
            pltpu.SemaphoreType.DMA((2, 5, 4)),
            pltpu.SemaphoreType.DMA((2, 5, 4)),
            pltpu.SemaphoreType.DMA((2, 5, 4)),
            pltpu.SemaphoreType.DMA((2, 16)),
            pltpu.SemaphoreType.DMA((2, 16)),
            pltpu.SemaphoreType.DMA((2, NZ)),
            pltpu.SemaphoreType.DMA((2, NZ)),
            pltpu.SemaphoreType.DMA((2, NZ)),
            pltpu.SemaphoreType.DMA((2, NZ)),
        ],
        compiler_params=pltpu.CompilerParams(
            collective_id=0, has_side_effects=True, vmem_limit_bytes=40 * 1024 * 1024
        ),
        name="graph_conv",
    )(*(pltpu.with_memory_space_constraint(v, pltpu.HBM) for v in (
        features,
        proj_weight,
        jnp.transpose(source_block, (1, 2, 0)),
        jnp.transpose(slot_count, (1, 0)),
        block_pattern,
        node_type.reshape(1, BLK),
        type_gain,
        cotangent,
    )))
    activations, grad = pl.pallas_call(
        finish,
        out_shape=(
            jax.ShapeDtypeStruct((BLK, HID), BF16),
            jax.ShapeDtypeStruct((REL * BLK, HID), F32),
        ),
        in_specs=[vmem, vmem],
        out_specs=(vmem, vmem),
        compiler_params=pltpu.CompilerParams(vmem_limit_bytes=4 * 1024 * 1024),
        name="finish",
    )(activations, parts)
    return activations, grad.reshape(REL, BLK, HID)


def solution(mesh):
    placed = (
        P("dom", "feat"),
        P(None, "feat", None),
        P("dom", None, None),
        P("dom", None),
        P("dom", None, None, None, None),
        P(("dom", "feat")),
        P(),
        P(("dom", "feat"), None),
    )
    return jax.shard_map(
        body,
        mesh=mesh,
        in_specs=placed,
        out_specs=(P(("dom", "feat"), None), P(None, "feat", None)),
        check_vma=False,
    )
```

```python
import functools

import jax
import jax.numpy as jnp
from jax import lax
from jax.experimental import pallas as pl
from jax.experimental.pallas import tpu as pltpu
from jax.sharding import PartitionSpec as P

MESH = pl.DeviceIdType.MESH
F32 = jnp.float32
BF16 = jnp.bfloat16
BLK = 128
REL = 3
NTYPES = 3
SLOTS = 4
PB = 32
HID = 256
NZ = 8
DXS = (2, 3, 1, 0)
PART = REL * BLK // NZ


def kernel(
    feat_hbm,
    weight_hbm,
    source_hbm,
    count_hbm,
    pattern_hbm,
    type_hbm,
    gain_hbm,
    cot_hbm,
    act_ref,
    wg_all,
    feat_ref,
    weight_ref,
    source_ref,
    count_ref,
    pattern_ref,
    type_ref,
    gain_ref,
    cot_ref,
    load_sem,
    self_t,
    perm_t,
    weight_t,
    mixed_t,
    own_part,
    keep_top,
    pair_out,
    pair_in,
    x_out,
    x_in,
    y_out,
    y_in,
    turn_out,
    turn_in,
    slope_all,
    grad_acc,
    wg_out,
    wg_in,
    pair_send,
    pair_recv,
    x_send,
    x_recv,
    y_send,
    y_recv,
    turn_send,
    turn_recv,
    agx_send,
    agx_recv,
    agy_send,
    agy_recv,
    core_send,
    core_recv,
    zs_send,
    zs_recv,
    zb_send,
    zb_recv,
):
    dom = lax.axis_index("dom")
    me = lax.axis_index("feat")
    core = me % 2
    chip = me // 2
    x = chip % 4
    y = chip // 4
    partner = me + 1 - 2 * core

    def at_feat(dest):
        return (dom, dest)

    def device_at(dy, dx):
        return (((y + dy) % 4) * 4 + (x + dx) % 4) * 2 + core

    def piece_of(ref, n):
        return ref.at[pl.ds(n * 1024, 1024)]

    loads = [
        pltpu.make_async_copy(src, dst, load_sem.at[n])
        for n, (src, dst) in enumerate((
            (piece_of(feat_hbm, 0), piece_of(feat_ref, 0)),
            (piece_of(feat_hbm, 1), piece_of(feat_ref, 1)),
            (piece_of(feat_hbm, 2), piece_of(feat_ref, 2)),
            (piece_of(feat_hbm, 3), piece_of(feat_ref, 3)),
            (weight_hbm, weight_ref),
            (source_hbm, source_ref),
            (count_hbm, count_ref),
            (pattern_hbm, pattern_ref),
            (type_hbm, type_ref),
            (gain_hbm, gain_ref),
            (cot_hbm, cot_ref),
        ))
    ]
    for load in loads:
        load.start()

    barrier = pltpu.get_barrier_semaphore()

    def greet(dest):
        pl.semaphore_signal(barrier, inc=1, device_id=dest, device_id_type=MESH)

    greet(at_feat(partner))
    for d in range(1, 4):
        greet(at_feat(device_at(0, d)))
        greet(at_feat(device_at(d, 0)))
    for dz in range(1, NZ):
        greet(((dom + dz) % NZ, me))

    row = lax.broadcasted_iota(jnp.int32, (BLK, BLK), 0)
    col = lax.broadcasted_iota(jnp.int32, (BLK, BLK), 1)
    scale = 1.0 / (jnp.int32(1) << (col // 8)).astype(F32)
    perm = jnp.where(row == (col % 8) * 16 + col // 8, scale, 0.0).astype(BF16)
    eye = jnp.where(row == col, 1.0, 0.0).astype(BF16)

    for n in range(4):
        loads[n].wait()
        flipped = lax.dot_general(
            eye,
            feat_ref[n * 1024:(n + 1) * 1024],
            (((1,), (1,)), ((), ())),
            preferred_element_type=F32,
        ).astype(BF16)
        blocks = [flipped[:, k * BLK:(k + 1) * BLK] for k in range(8)]
        for k in range(8):
            self_t[n * 8 + k] = blocks[k]
        moved = jnp.dot(jnp.concatenate(blocks, axis=0), perm, preferred_element_type=F32)
        perm_t[n * 8:(n + 1) * 8] = moved.astype(BF16).reshape(8, BLK, BLK)
    loads[4].wait()
    for r in range(REL):
        for half in range(2):
            piece = weight_ref[r, :, half * BLK:(half + 1) * BLK]
            weight_t[half * BLK:(half + 1) * BLK, r * BLK:(r + 1) * BLK] = (
                piece.astype(F32).T.astype(BF16)
            )
    for load in loads[5:]:
        load.wait()

    def mix(b):
        own_rows = self_t[b].astype(F32)
        for r in range(REL):
            count = count_ref[r, b]
            tiles = []
            gathered = []
            degree = None
            for s in range(SLOTS):
                words = pattern_ref[b, r, s]
                if s > 0:
                    words = words & jnp.where(s < count, jnp.int32(65535), jnp.int32(0))
                bits = lax.population_count(words)
                degree = bits if degree is None else degree + bits
                for j in range(16):
                    tiles.append((words & (1 << j)).astype(F32))
                gathered.append(perm_t[source_ref[r, s, b]])
            adj = jnp.concatenate(tiles, axis=0).astype(BF16)
            sources = jnp.concatenate(gathered, axis=1)
            summed = jnp.dot(sources, adj, preferred_element_type=F32)
            total = 1.0 + jnp.sum(degree.astype(F32), axis=0, keepdims=True)
            mixed_t[b, r * BLK:(r + 1) * BLK, :] = ((own_rows + summed) * (1.0 / total)).astype(BF16)

    def pair_copy(step):
        return pltpu.make_async_remote_copy(
            src_ref=pair_out.at[step],
            dst_ref=pair_in.at[step],
            send_sem=pair_send.at[step],
            recv_sem=pair_recv.at[step],
            device_id=at_feat(partner),
            device_id_type=MESH,
        )

    def shift(n):
        return 2 + n - 3 * (n // 2) - 2 * (n // 3)

    def offset(step):
        group, k = step // 4, step % 4
        return shift(group), shift(k)

    def target(step):
        dy, dx = offset(step)
        return device_at(dy, dx)

    def x_copy(step, dx):
        return pltpu.make_async_remote_copy(
            src_ref=x_out.at[step],
            dst_ref=x_in.at[step],
            send_sem=x_send.at[step],
            recv_sem=x_recv.at[step],
            device_id=at_feat(device_at(0, dx)),
            device_id_type=MESH,
        )

    def y_copy(step, dy):
        return pltpu.make_async_remote_copy(
            src_ref=y_out.at[step],
            dst_ref=y_in.at[step],
            send_sem=y_send.at[step],
            recv_sem=y_recv.at[step],
            device_id=at_feat(device_at(dy, 0)),
            device_id_type=MESH,
        )

    def turn_copy(kind, slot, d):
        return pltpu.make_async_remote_copy(
            src_ref=turn_out.at[kind, slot],
            dst_ref=turn_in.at[kind, slot],
            send_sem=turn_send.at[kind, slot],
            recv_sem=turn_recv.at[kind, slot],
            device_id=at_feat(device_at(d, 0) if kind == 0 else device_at(0, d)),
            device_id_type=MESH,
        )

    def mix_both(step):
        mine = target(step)
        mix(mine)
        mix(mine + 1 - 2 * core)

    def project(step):
        mine = target(step)
        other = mine + 1 - 2 * core
        both = jnp.concatenate([mixed_t[mine], mixed_t[other]], axis=1)
        part = jnp.dot(weight_t[...], both, preferred_element_type=F32)
        own_part[step] = part[:, :BLK]
        pair_out[step] = part[:, BLK:].astype(BF16)

    def top_sum(step):
        return own_part[step, :BLK] + pair_in[step, :BLK].astype(F32)

    def low_sum(step):
        return own_part[step, BLK:] + pair_in[step, BLK:].astype(F32)

    def send_top(step, k):
        x_out[step] = top_sum(step).astype(BF16)
        x_copy(step, DXS[k]).start()

    def send_low(step, dy):
        y_out[step] = low_sum(step).astype(BF16)
        y_copy(step, dy).start()

    def row_sum(group, mine):
        for k in range(3):
            x_copy(4 * group + k, DXS[k]).wait_recv()
            mine = mine + x_in[4 * group + k].astype(F32)
        return mine

    def send_row(group, dy):
        turn_out[0, group] = row_sum(group, keep_top[group]).astype(BF16)
        turn_copy(0, group, dy).start()

    def column_sum(k, mine):
        for group in range(3):
            y_copy(4 * group + k, 1).wait_recv()
            mine = mine + y_in[4 * group + k].astype(F32)
        return mine

    pl.semaphore_wait(barrier, 1 + 6 + NZ - 1)
    mix_both(0)
    project(0)
    mix_both(1)
    pair_copy(0).start()
    project(1)
    mix_both(2)
    pair_copy(1).start()

    def four(group, carry):
        dy = shift(group)
        for k in range(4):
            step = 4 * group + k
            project(step + 2)
            mix_both(step + 3)
            pair_copy(step + 2).start()
            pair_copy(step).wait_recv()
            if k < 3:
                send_top(step, k)
            else:
                keep_top[group] = top_sum(step)
            send_low(step, dy)
            if k == 2:
                @pl.when(group > 0)
                def _():
                    send_row(group - 1, shift(group - 1))
        return carry

    lax.fori_loop(0, 3, four, 0)
    for k in range(4):
        step = 12 + k
        if k < 2:
            project(step + 2)
            if k < 1:
                mix_both(step + 3)
            pair_copy(step + 2).start()
        pair_copy(step).wait_recv()
        if k < 3:
            send_top(step, k)
            turn_out[1, k] = column_sum(k, low_sum(step)).astype(BF16)
            turn_copy(1, k, DXS[k]).start()
        if k == 2:
            send_row(2, 1)
    def to_core(half, block, slot):
        return pltpu.make_async_remote_copy(
            src_ref=slope_all.at[half, block],
            dst_ref=slope_all.at[half, block],
            send_sem=core_send.at[half, slot],
            recv_sem=core_recv.at[half, slot],
            device_id=at_feat(partner),
            device_id_type=MESH,
        )

    def over_x(half, block, line, dx):
        rows = pl.ds(64 if line > 0 else 0, 64)
        return pltpu.make_async_remote_copy(
            src_ref=slope_all.at[half, block, rows],
            dst_ref=slope_all.at[half, block, rows],
            send_sem=agx_send.at[half, line, dx],
            recv_sem=agx_recv.at[half, line, dx],
            device_id=at_feat(device_at(0, dx)),
            device_id_type=MESH,
        )

    def over_y(half, block, line, dy):
        rows = pl.ds(0 if line > 0 else 64, 64)
        return pltpu.make_async_remote_copy(
            src_ref=slope_all.at[half, block, rows],
            dst_ref=slope_all.at[half, block, rows],
            send_sem=agy_send.at[half, line, dy],
            recv_sem=agy_recv.at[half, line, dy],
            device_id=at_feat(device_at(dy, 0)),
            device_id_type=MESH,
        )

    types = jnp.broadcast_to(type_ref[...].astype(F32), (BLK, BLK)).T
    for half in range(2):
        total = row_sum(3, top_sum(15)) if half == 0 else column_sum(3, low_sum(15))
        for slot in range(3):
            turn_copy(half, slot, 1).wait_recv()
            total = total + turn_in[half, slot].astype(F32)
        cols = slice(half * BLK, (half + 1) * BLK)
        pre = total.T
        gains = gain_ref[:, cols]
        gain = jnp.where(types == 0.0, gains[0:1], jnp.where(types == 1.0, gains[1:2], gains[2:3]))
        sig = jax.nn.sigmoid(pre)
        slope = cot_ref[:, cols].astype(F32) * gain * (sig * (1.0 + pre * (1.0 - sig)))
        slope_all[half, me] = slope.astype(BF16)
        act_ref[:, cols] = (pre * sig * gain).astype(BF16)
        for line in range(2):
            for d in DXS[:3]:
                over_x(half, me, line, d).start()
                over_y(half, me, line, d).start()
        to_core(half, me, 0).start()

    def forward(half):
        for d in (1, 3, 2):
            across = device_at(0, 4 - d)
            over_x(half, across, 0, d).wait_recv()
            for e in DXS[:3]:
                over_y(half, across, 1 + d, e).start()
            down = device_at(4 - d, 0)
            over_y(half, down, 0, d).wait_recv()
            for e in DXS[:3]:
                over_x(half, down, 1 + d, e).start()

    def arrived(half, dy, dx):
        block = device_at(4 - dy, 4 - dx)
        if dx > 0:
            over_x(half, block, 1 + dy, dx).wait_recv()
        if dy > 0:
            over_y(half, block, 1 + dx, dy).wait_recv()
        return block

    order = [(0, 1), (0, 3), (1, 0), (3, 0), (0, 2), (2, 0), (1, 1), (1, 3), (3, 1), (3, 3),
             (1, 2), (2, 1), (3, 2), (2, 3), (2, 2)]

    places = [(0, 0)] + order

    def relay(half, chunk):
        for dy, dx in places[4 * chunk:4 * chunk + 4]:
            if (dy, dx) != (0, 0):
                to_core(half, arrived(half, dy, dx), dy * 4 + dx).start()

    def multiply(half, chunk):
        lhs, rhs = [], []
        for dy, dx in places[4 * chunk:4 * chunk + 4]:
            block = device_at((4 - dy) % 4, (4 - dx) % 4)
            twin = block + 1 - 2 * core
            to_core(half, twin, dy * 4 + dx).wait_recv()
            lhs += [mixed_t[block], mixed_t[twin]]
            rhs += [slope_all[half, block], slope_all[half, twin]]
        product = jnp.dot(
            jnp.concatenate(lhs, axis=1),
            jnp.concatenate(rhs, axis=0),
            preferred_element_type=F32,
        )
        if chunk == 0:
            grad_acc[...] = product
        else:
            grad_acc[...] += product

    def gradient(half):
        relay(half, 0)
        for chunk in range(4):
            if chunk < 3:
                relay(half, chunk + 1)
            multiply(half, chunk)

    def scatter(half, dz):
        return pltpu.make_async_remote_copy(
            src_ref=wg_out.at[half, (dom + dz) % NZ],
            dst_ref=wg_in.at[half, dz],
            send_sem=zs_send.at[half, dz],
            recv_sem=zs_recv.at[half, dz],
            device_id=((dom + dz) % NZ, me),
            device_id_type=MESH,
        )

    def spread(half, dz, part):
        return pltpu.make_async_remote_copy(
            src_ref=wg_all.at[half, part],
            dst_ref=wg_all.at[half, part],
            send_sem=zb_send.at[half, dz],
            recv_sem=zb_recv.at[half, dz],
            device_id=((dom + dz) % NZ, me),
            device_id_type=MESH,
        )

    zorder = (4, 3, 5, 2, 6, 1, 7)

    def scatter_all(half):
        for p in range(NZ):
            wg_out[half, p] = grad_acc[p * PART:(p + 1) * PART, :].astype(BF16)
        for dz in zorder:
            scatter(half, dz).start()
        return grad_acc[pl.ds(pl.multiple_of(dom * PART, 8), PART), :]

    def spread_all(half, own):
        for dz in reversed(zorder):
            scatter(half, dz).wait_recv()
            own = own + wg_in[half, dz].astype(F32)
        wg_all[half, dom] = own.astype(BF16)
        for dz in zorder:
            spread(half, dz, dom).start()

    forward(0)
    forward(1)
    gradient(0)
    first = scatter_all(0)
    gradient(1)
    second = scatter_all(1)
    spread_all(0, first)
    spread_all(1, second)

    def drain(step, carry):
        pair_copy(step).wait_send()
        return carry

    lax.fori_loop(0, 16, drain, 0)
    for step in range(16):
        if step % 4 < 3:
            x_copy(step, 1).wait_send()
        if step < 12:
            y_copy(step, 1).wait_send()
    for slot in range(3):
        turn_copy(0, slot, 1).wait_send()
        turn_copy(1, slot, 1).wait_send()
    for half in range(2):
        for d in range(1, 4):
            for line in range(5):
                over_x(half, me, line, d).wait_send()
                over_y(half, me, line, d).wait_send()
        for slot in range(16):
            to_core(half, me, slot).wait_send()
        for dz in range(1, NZ):
            scatter(half, dz).wait_send()
            spread(half, dz, dom).wait_send()
    for half in range(2):
        for dz in range(1, NZ):
            spread(half, dz, (dom + NZ - dz) % NZ).wait_recv()


def finish(act_in, wg_in, act_ref, grad_ref):
    act_ref[...] = act_in[...]
    for half in range(2):
        for p in range(NZ):
            grad_ref[p * PART:(p + 1) * PART, half * BLK:(half + 1) * BLK] = wg_in[half, p].astype(F32)


def body(
    features, proj_weight, source_block, slot_count, block_pattern, node_type, type_gain, cotangent
):
    vmem = pl.BlockSpec(memory_space=pltpu.VMEM)
    activations, parts = pl.pallas_call(
        kernel,
        out_shape=(
            jax.ShapeDtypeStruct((BLK, HID), BF16),
            jax.ShapeDtypeStruct((2, NZ, PART, BLK), BF16),
        ),
        in_specs=[pl.BlockSpec(memory_space=pltpu.HBM)] * 8,
        out_specs=(vmem, vmem),
        scratch_shapes=[
            pltpu.VMEM((PB * BLK, BLK), BF16),
            pltpu.VMEM((REL, BLK, HID), BF16),
            pltpu.SMEM((REL, SLOTS, PB), jnp.int32),
            pltpu.SMEM((REL, PB), jnp.int32),
            pltpu.VMEM((PB, REL, SLOTS, 8, BLK), jnp.int32),
            pltpu.VMEM((1, BLK), jnp.int32),
            pltpu.VMEM((NTYPES, HID), F32),
            pltpu.VMEM((BLK, HID), BF16),
            pltpu.SemaphoreType.DMA((11,)),
            pltpu.VMEM((PB, BLK, BLK), BF16),
            pltpu.VMEM((PB, BLK, BLK), BF16),
            pltpu.VMEM((HID, REL * BLK), BF16),
            pltpu.VMEM((PB, REL * BLK, BLK), BF16),
            pltpu.VMEM((16, HID, BLK), F32),
            pltpu.VMEM((3, BLK, BLK), F32),
            pltpu.VMEM((16, HID, BLK), BF16),
            pltpu.VMEM((16, HID, BLK), BF16),
            pltpu.VMEM((16, BLK, BLK), BF16),
            pltpu.VMEM((16, BLK, BLK), BF16),
            pltpu.VMEM((16, BLK, BLK), BF16),
            pltpu.VMEM((16, BLK, BLK), BF16),
            pltpu.VMEM((2, 3, BLK, BLK), BF16),
            pltpu.VMEM((2, 3, BLK, BLK), BF16),
            pltpu.VMEM((2, PB, BLK, BLK), BF16),
            pltpu.VMEM((REL * BLK, BLK), F32),
            pltpu.VMEM((2, NZ, PART, BLK), BF16),
            pltpu.VMEM((2, NZ, PART, BLK), BF16),
            pltpu.SemaphoreType.DMA((16,)),
            pltpu.SemaphoreType.DMA((16,)),
            pltpu.SemaphoreType.DMA((16,)),
            pltpu.SemaphoreType.DMA((16,)),
            pltpu.SemaphoreType.DMA((16,)),
            pltpu.SemaphoreType.DMA((16,)),
            pltpu.SemaphoreType.DMA((2, 3)),
            pltpu.SemaphoreType.DMA((2, 3)),
            pltpu.SemaphoreType.DMA((2, 5, 4)),
            pltpu.SemaphoreType.DMA((2, 5, 4)),
            pltpu.SemaphoreType.DMA((2, 5, 4)),
            pltpu.SemaphoreType.DMA((2, 5, 4)),
            pltpu.SemaphoreType.DMA((2, 16)),
            pltpu.SemaphoreType.DMA((2, 16)),
            pltpu.SemaphoreType.DMA((2, NZ)),
            pltpu.SemaphoreType.DMA((2, NZ)),
            pltpu.SemaphoreType.DMA((2, NZ)),
            pltpu.SemaphoreType.DMA((2, NZ)),
        ],
        compiler_params=pltpu.CompilerParams(
            collective_id=0, has_side_effects=True, vmem_limit_bytes=40 * 1024 * 1024
        ),
        name="graph_conv",
    )(*(pltpu.with_memory_space_constraint(v, pltpu.HBM) for v in (
        features,
        proj_weight,
        jnp.transpose(source_block, (1, 2, 0)),
        jnp.transpose(slot_count, (1, 0)),
        block_pattern,
        node_type.reshape(1, BLK),
        type_gain,
        cotangent,
    )))
    activations, grad = pl.pallas_call(
        finish,
        out_shape=(
            jax.ShapeDtypeStruct((BLK, HID), BF16),
            jax.ShapeDtypeStruct((REL * BLK, HID), F32),
        ),
        in_specs=[vmem, vmem],
        out_specs=(vmem, vmem),
        compiler_params=pltpu.CompilerParams(vmem_limit_bytes=4 * 1024 * 1024),
        name="finish",
    )(activations, parts)
    return activations, grad.reshape(REL, BLK, HID)


def solution(mesh):
    placed = (
        P("dom", "feat"),
        P(None, "feat", None),
        P("dom", None, None),
        P("dom", None),
        P("dom", None, None, None, None),
        P(("dom", "feat")),
        P(),
        P(("dom", "feat"), None),
    )
    return jax.shard_map(
        body,
        mesh=mesh,
        in_specs=placed,
        out_specs=(P(("dom", "feat"), None), P(None, "feat", None)),
        check_vma=False,
    )
```
